128 devices in a mesh: lon: 8 (over x_lo, y), lat: 16 (over z, x_hi, core).
Axes of the slice: x: 4 (x_hi: 2, x_lo: 2; x = x_hi * 2 + x_lo), y: 4, z: 4, core: 2. Of those that a mesh axis runs over, the one named last changes fastest.
Arguments:
- velocity: float32 [3, 128, 192, 384], P(None, 'lon', 'lat'), may hold values from -6 to 6
- pressure_in: float32 [128, 192, 384], P('lon', 'lat')
- viscosity: float32 [128, 192, 384], P('lon', 'lat'), as said below
- body_force: float32 [3, 128, 192, 384], P(None, 'lon', 'lat'), may hold values from -60 to 60
- colour_order: int32 [8], replicated, may hold values from 0 to 7, each once
Outputs:
- velocity_out: float32 [3, 128, 192, 384], P(None, 'lon', 'lat')
- pressure_out: float32 [128, 192, 384], P('lon', 'lat')
The draws below stay inside these ranges and needn't reach their ends.
Inputs may be any that keep to these rules, and one draw needn't show every extreme that they name: colour_order names each of the 8 colours once. viscosity lies between 1 and 1000000.
All inputs are finite; a program needn't handle non-finite values.
Results may differ from the reference program's by a relative error of at most 0.0003.
Values sent between devices are 32-bit elements; how exact they have to be, the bound alone decides.
A program may use at most 320 MiB of HBM per device.

```python
import math
import jax
import jax.numpy as jnp
from jax import lax

SWEEPS = 2
COLOURS = 8
NX = 128
NY = 192
NZ = 384


def shared_viscosity(key):
    viscous_key = jax.random.fold_in(key, 11)
    exponent = jax.random.uniform(viscous_key, (NX, NY, NZ), jnp.float32, 0.0, math.log(1000000.0))
    return jnp.exp(exponent)


def shared_pressure(key):
    wave_key = jax.random.fold_in(key, 23)
    noise_key = jax.random.fold_in(key, 37)
    phases = jax.random.uniform(jax.random.fold_in(wave_key, 1), (3,), jnp.float32, 0.0, 2.0 * math.pi)
    factors = jax.random.uniform(jax.random.fold_in(wave_key, 2), (3,), jnp.float32, 0.5, 1.0)
    lon_pos = jnp.arange(NX).astype(jnp.float32)
    lat_pos = jnp.arange(NY).astype(jnp.float32)
    rad_pos = jnp.arange(NZ).astype(jnp.float32)
    lon_wave = factors[0] * 10.0 * NX / (2.0 * math.pi) * jnp.cos(2.0 * math.pi * lon_pos / NX + phases[0])
    lat_wave = factors[1] * 10.0 * NY / (2.0 * math.pi) * jnp.cos(math.pi * lat_pos / NY + phases[1])
    rad_wave = factors[2] * 10.0 * NZ / (2.0 * math.pi) * jnp.cos(math.pi * rad_pos / NZ + phases[2])
    smooth_part = lon_wave[:, None, None] + lat_wave[None, :, None] + rad_wave[None, None, :]
    noise = 3.0 * jax.random.normal(noise_key, (NX, NY, NZ), jnp.float32)
    return smooth_part + noise


def draw_viscosity(key, part):
    return shared_viscosity(key)


def draw_pressure_in(key, part):
    return shared_pressure(key) / shared_viscosity(key)


def block_scale(own_key, shape, cuts, least, top_value):
    level = 1.0
    for position, blocks in cuts:
        steps = jax.random.uniform(jax.random.fold_in(jax.random.fold_in(own_key, 6), position), (blocks,), jnp.float32, least / len(cuts), top_value / len(cuts))
        level = level * jnp.repeat(jnp.exp(steps), shape[position] // blocks).reshape((-1,) + (1,) * (len(shape) - 1 - position))
    return level


def normal_values(own_key, shape, scale, most, cuts=(), kind=jnp.bfloat16):
    array = jax.random.normal(own_key, shape, jnp.float32) * scale
    if len(cuts) > 0:
        array = block_scale(own_key, shape, cuts, -0.22, 0.18) * array
    return jnp.clip(array, min=-most, max=most).astype(kind)


def setup_inputs(seed: int = 0) -> dict:
    splits = jax.random.split(jax.random.key(seed), 6)
    velocity = normal_values(splits[0], (3, NX, NY, NZ), 1.0, 6.0, ((1, 8), (2, 16)), jnp.float32)
    pressure_in = draw_pressure_in(jax.random.fold_in(splits[5], 71), 0)
    viscosity = draw_viscosity(jax.random.fold_in(splits[5], 71), 0)
    body_force = normal_values(splits[3], (3, NX, NY, NZ), 10.0, 60.0, ((1, 8), (2, 16)), jnp.float32)
    colour_order = jax.random.permutation(splits[4], COLOURS).astype(jnp.int32)
    return dict(velocity=velocity, pressure_in=pressure_in, viscosity=viscosity, body_force=body_force, colour_order=colour_order)


damping = 0.6
coarse_gain = 0.25
unit_steps = ((1, 0, 0), (0, 1, 0), (0, 0, 1))


def stencil_offsets():
    result = []
    for step_x in (-1, 0, 1):
        for step_y in (-1, 0, 1):
            for step_z in (-1, 0, 1):
                reach = abs(step_x) + abs(step_y) + abs(step_z)
                if reach > 0:
                    result.append((step_x, step_y, step_z, 0.5 ** (reach - 1)))
    return result


def slide(values, offset, axis_no):
    if offset == 0:
        return values
    extent = values.shape[axis_no]
    padding = [(0, 0)] * values.ndim
    if offset > 0:
        padding[axis_no] = (0, offset)
        return lax.slice_in_dim(jnp.pad(values, padding), offset, offset + extent, axis=axis_no)
    padding[axis_no] = (-offset, 0)
    return lax.slice_in_dim(jnp.pad(values, padding), 0, extent, axis=axis_no)


def moved(values, step_x, step_y, step_z):
    base = values.ndim - 3
    result = values
    if step_x != 0:
        result = jnp.roll(result, -step_x, axis=base)
    result = slide(result, step_y, base + 1)
    return slide(result, step_z, base + 2)


def blend(own_value, next_value):
    return 2.0 * own_value * next_value / (own_value + next_value)


def viscous_diagonal(viscous):
    running = jnp.zeros_like(viscous)
    for step_x, step_y, step_z, weight in stencil_offsets():
        running = running + weight * blend(viscous, moved(viscous, step_x, step_y, step_z))
    return running


def residuals(fields, viscous, diagonal, body_force):
    velocity = fields[:3]
    pressure = fields[3]
    applied = diagonal * velocity
    for step_x, step_y, step_z, weight in stencil_offsets():
        coupling = weight * blend(viscous, moved(viscous, step_x, step_y, step_z))
        applied = applied - coupling * moved(velocity, step_x, step_y, step_z)
    gradient = jnp.stack([moved(pressure, -unit_step[0], -unit_step[1], -unit_step[2]) - pressure for unit_step in unit_steps])
    momentum = body_force - applied - gradient
    continuity = jnp.zeros_like(pressure)
    for axis_no, unit_step in enumerate(unit_steps):
        continuity = continuity - (moved(velocity[axis_no], unit_step[0], unit_step[1], unit_step[2]) - velocity[axis_no])
    return momentum, continuity


def colour_step(fields, viscous, diagonal, inverse, weight_sum, body_force, chosen):
    momentum, continuity = residuals(fields, viscous, diagonal, body_force)
    scaled = momentum * inverse
    mismatch = -continuity
    for axis_no, unit_step in enumerate(unit_steps):
        mismatch = mismatch + moved(scaled[axis_no], unit_step[0], unit_step[1], unit_step[2]) - scaled[axis_no]
    change = chosen * mismatch / weight_sum
    updates = []
    for axis_no, unit_step in enumerate(unit_steps):
        before = moved(chosen, -unit_step[0], -unit_step[1], -unit_step[2])
        earlier = moved(change, -unit_step[0], -unit_step[1], -unit_step[2])
        updates.append(inverse * ((chosen + before) * momentum[axis_no] + change - earlier))
    velocity = fields[:3] + damping * jnp.stack(updates)
    pressure = fields[3] + damping * change
    return jnp.concatenate([velocity, pressure[None]], axis=0)


def colour_codes(shape):
    lon_parity = jnp.arange(shape[0], dtype=jnp.int32) % 2
    lat_parity = jnp.arange(shape[1], dtype=jnp.int32) % 2
    rad_parity = jnp.arange(shape[2], dtype=jnp.int32) % 2
    return lon_parity[:, None, None] + 2 * lat_parity[None, :, None] + 4 * rad_parity[None, None, :]


def reference(velocity, pressure_in, viscosity, body_force, colour_order):
    diagonal = viscous_diagonal(viscosity)
    inverse = 1.0 / diagonal
    weight_sum = 3.0 * inverse
    for unit_step in unit_steps:
        weight_sum = weight_sum + moved(inverse, unit_step[0], unit_step[1], unit_step[2])
    parity_code = colour_codes(viscosity.shape)
    fields = jnp.concatenate([velocity, (pressure_in * viscosity)[None]], axis=0)

    def sweep(sweep_no, current):
        colour = colour_order[sweep_no % COLOURS]
        chosen = (parity_code == colour).astype(jnp.float32)
        return colour_step(current, viscosity, diagonal, inverse, weight_sum, body_force, chosen)

    fields = lax.fori_loop(0, SWEEPS * COLOURS, sweep, fields)
    momentum, continuity = residuals(fields, viscosity, diagonal, body_force)
    cycle_cells = NX // 8
    summed = momentum.reshape(3, cycle_cells, 8, NY // 4, 4, NZ // 4, 4).sum(axis=(2, 4, 6))
    viscous_sum = viscosity.reshape(cycle_cells, 8, NY // 4, 4, NZ // 4, 4).sum(axis=(1, 3, 5))
    coarse = summed / viscous_sum[None]
    decay_rate = 4.0 / cycle_cells
    screening = 2.0 * math.cosh(decay_rate) - 2.0
    angles = 2.0 * math.pi * jnp.arange(cycle_cells).astype(jnp.float32) / cycle_cells
    symbol = screening / (screening + 2.0 - 2.0 * jnp.cos(angles))
    spectrum = jnp.fft.fft(coarse, axis=1) * symbol[None, :, None, None]
    smooth = jnp.real(jnp.fft.ifft(spectrum, axis=1))
    spread = jnp.repeat(jnp.repeat(jnp.repeat(smooth, 8, axis=1), 4, axis=2), 4, axis=3)
    velocity_out = fields[:3] + coarse_gain * spread
    pressure_out = fields[3] / viscosity
    return velocity_out, pressure_out
```

```python
import functools
import math

import jax
import jax.numpy as jnp
from jax import lax
from jax.experimental import pallas as pl
from jax.experimental.pallas import tpu as pltpu
from jax.sharding import PartitionSpec as P

SWEEPS = 2
COLOURS = 8
STEPS = SWEEPS * COLOURS
DAMP = 0.6
GAIN = 0.25
NEW = 6
FIRST = 16
MESH = pl.DeviceIdType.MESH
DIRECTIONS = ((1, 0), (-1, 0), (0, 1), (0, -1), (1, 1), (1, -1), (-1, 1), (-1, -1))


def opposite(n):
    return DIRECTIONS.index((-DIRECTIONS[n][0], -DIRECTIONS[n][1]))


def kslot(dx, dy, dz):
    return ((dx + 1) * 3 + (dy + 1)) * 3 + (dz + 1)


def cycle_kernel(cells):
    rate = 4.0 / cells
    screening = 2.0 * math.cosh(rate) - 2.0
    factor = screening / (2.0 * math.sinh(rate) * math.sinh(rate * cells / 2.0))
    return [factor * math.cosh(rate * (cells / 2.0 - d)) for d in range(cells)]


def kernel(
    lon_n,
    lat_n,
    order_ref,
    vis,
    force,
    start_ref,
    vel_out,
    p_out,
    slots,
    coup,
    diag,
    inv,
    winv,
    send_x,
    send_y,
    send_c,
    recv_x,
    recv_y,
    recv_c,
    gathered,
    shared,
    load_sem,
    send_sem,
    recv_sem,
    gsend_sem,
    grecv_sem,
):
    lon = lax.axis_index("lon")
    lat = lax.axis_index("lat")
    planes = vis.shape[0]
    depth = vis.shape[-1]
    blocks = planes // 2 - 2
    tile = (8, depth)
    rows = lax.broadcasted_iota(jnp.int32, tile, 0)
    lanes = lax.broadcasted_iota(jnp.int32, tile, 1)

    def roll_rows(v, up):
        return pltpu.roll(v, up % 8, 0)

    def roll_lanes(v, up):
        return pltpu.roll(v, up % depth, 1)

    def above_z(v):
        return jnp.where(lanes == depth - 1, 0.0, roll_lanes(v, -1))

    def below_z(v):
        return jnp.where(lanes == 0, 0.0, roll_lanes(v, 1))

    def partner(n):
        dx, dy = DIRECTIONS[n]
        return (lax.rem(lon + dx + lon_n, lon_n), lat + dy)

    def present(n):
        dy = DIRECTIONS[n][1]
        if dy > 0:
            return lat < lat_n - 1
        if dy < 0:
            return lat > 0
        return None

    def guarded(cond, fn):
        if cond is None:
            fn()
        else:
            pl.when(cond)(fn)

    load = pltpu.make_async_copy(
        start_ref, slots.at[pl.ds(0, FIRST), pl.ds(1, blocks + 2)], load_sem
    )
    load.start()
    load.wait()

    barrier = pltpu.get_barrier_semaphore()
    for n in range(8):

        def greet(n=n):
            pl.semaphore_signal(barrier, inc=1, device_id=partner(n), device_id_type=MESH)

        guarded(present(n), greet)
    for hop in range(2, lon_n - 1):
        pl.semaphore_signal(
            barrier, inc=1, device_id=(lax.rem(lon + hop, lon_n), lat), device_id_type=MESH
        )
    ends = (lat == 0).astype(jnp.int32) + (lat == lat_n - 1).astype(jnp.int32)
    pl.semaphore_wait(barrier, lon_n + 5 - 3 * ends)

    def inside(yp):
        y = lat * 12 + 2 * (rows - 1) + yp
        return (y >= 0) & (y < 12 * lat_n)

    half = [(1, dy, dz) for dy in (-1, 0, 1) for dz in (-1, 0, 1)]
    half += [(0, 1, dz) for dz in (-1, 0, 1)] + [(0, 0, 1)]

    def couple(x, carry):
        for yp in (0, 1):
            own = vis[x, yp]
            for dx in (0, 1):
                for dy in (-1, 0, 1):
                    offsets = [o for o in half if o[0] == dx and o[1] == dy]
                    if not offsets:
                        continue
                    other_yp = yp if dy == 0 else 1 - yp
                    shift = 0
                    if dy == 1 and yp == 1:
                        shift = -1
                    if dy == -1 and yp == 0:
                        shift = 1
                    other = vis[x + dx, other_yp]
                    if shift:
                        other = roll_rows(other, shift)
                    for o in offsets:
                        dz = o[2]
                        beside = other
                        if dz == 1:
                            beside = above_z(other)
                        elif dz == -1:
                            beside = below_z(other)
                        reach = abs(dx) + abs(dy) + abs(dz)
                        scale = 2.0 * 0.5 ** (reach - 1)
                        value = (scale * own) * beside / jnp.maximum(own + beside, 1.0)
                        coup[kslot(*o), x, yp] = value
                        back = value
                        if dz:
                            back = roll_lanes(back, dz)
                        if shift:
                            back = roll_rows(back, -shift)
                        coup[kslot(-dx, -dy, -dz), x + dx, other_yp] = back
        return carry

    lax.fori_loop(1, planes - 1, couple, 0)

    def diagonal(x, carry):
        for yp in (0, 1):
            total = jnp.zeros(tile, jnp.float32)
            for n in range(27):
                if n != 13:
                    total = total + coup[n, x, yp]
            diag[x, yp] = total
            ok = inside(yp) & (total > 0)
            inv[x, yp] = jnp.where(ok, 1.0 / jnp.where(ok, total, 1.0), 0.0)
        return carry

    lax.fori_loop(2, planes - 1, diagonal, 0)

    def weights(x, carry):
        for yp in (0, 1):
            own = inv[x, yp]
            up = inv[x, 1 - yp]
            if yp == 1:
                up = roll_rows(up, -1)
            total = 3.0 * own + inv[x + 1, yp] + up + above_z(own)
            ok = inside(yp) & (total > 0)
            winv[x, yp] = jnp.where(ok, 1.0 / jnp.where(ok, total, 1.0), 0.0)
        return carry

    lax.fori_loop(2, planes - 2, weights, 0)

    def coupled(x, t, fields):
        at_low = t == 0

        def turn(v):
            return jnp.where(at_low, roll_rows(v, 1), roll_rows(v, -1))

        sums = [[None] * 3 for _ in fields]

        def gather(dy, yp, near):
            for dx in (-1, 0, 1):
                tiles = [f(dx, near) for f in fields]
                for dz in (-1, 0, 1):
                    if near and dx == 0 and dz == 0:
                        continue
                    k = coup[((1 - dx) * 3 + (1 - dy)) * 3 + (1 - dz), x + dx, yp]
                    for n, v in enumerate(tiles):
                        term = k * v
                        old = sums[n][dz + 1]
                        sums[n][dz + 1] = term if old is None else old + term

        gather(jnp.where(at_low, -1, 1), 1 - t, 0)
        for n in range(len(fields)):
            sums[n] = [turn(v) for v in sums[n]]
        gather(jnp.where(at_low, 1, -1), 1 - t, 0)
        gather(0, t, 1)
        return [s[1] + roll_lanes(s[2], -1) + roll_lanes(s[0], 1) for s in sums]

    def pick(table, xp, yp):
        low = jnp.where(yp == 0, table[0], table[1])
        high = jnp.where(yp == 0, table[2], table[3])
        return jnp.where(xp == 0, low, high)

    def sweep(s, table):
        colour = order_ref[lax.rem(s, COLOURS)]
        a = colour & 1
        b = (colour >> 1) & 1
        c = (colour >> 2) & 1
        base = FIRST + NEW * s
        side = s
        rel = {}
        for f in range(4):
            for xr in (0, 1):
                for yr in (0, 1):
                    rel[f, xr, yr] = pick(table[f * 4 : f * 4 + 4], a ^ xr, b ^ yr)
        shift = {
            (xr, yr): pick(table[16:20], a ^ xr, b ^ yr) for xr in (0, 1) for yr in (0, 1)
        }

        def field(f, xr, yr, block):
            index = block + 1
            if f == 0:
                index = index + shift[xr, yr]
            return slots[rel[f, xr, yr], index]

        zmask = (lanes & 1) == c
        z3 = (lanes > 0) | (c == 0)
        ymask = lat * 12 + 2 * (rows - 1) + (1 - b) >= 1
        low = b == 0

        def block_step(block, carry):
            x = 2 * block + a

            def main(f):
                def get(dx, near):
                    at = block if dx == 0 else (block - 1 + a if dx < 0 else block + a)
                    return field(f, abs(dx), 0 if near else 1, at)

                return get

            def xprime(dx, near):
                at = block + a if dx == 0 else (block if dx < 0 else block + 1)
                return field(0, 1 - abs(dx), 0 if near else 1, at)

            def yprime(dx, near):
                at = block if dx == 0 else (block - 1 + a if dx < 0 else block + a)
                return field(1, abs(dx), 1 if near else 0, at)

            p0 = field(3, 0, 0, block)
            p_x = field(3, 1, 0, block - 1 + a)
            p_x1 = field(3, 1, 0, block + a)
            p_y1 = field(3, 0, 1, block)
            k1, k2, k3 = coupled(x, b, [main(0), main(1), main(2)])
            own_inv = inv[x, b]
            p_y = jnp.where(low, roll_rows(p_y1, 1), p_y1)
            g1 = own_inv * (force[0, x, b] + k1 + (p0 - p_x))
            g2 = own_inv * (force[1, x, b] + k2 + (p0 - p_y))
            g3 = own_inv * (force[2, x, b] + k3 + (p0 - below_z(p0)))
            (kx,) = coupled(x + 1, b, [xprime])
            inv_x = inv[x + 1, b]
            gx = inv_x * (force[0, x + 1, b] + kx + (p_x1 - p0))
            (ky,) = coupled(x, 1 - b, [yprime])
            inv_y = inv[x, 1 - b]
            gy = inv_y * (force[1, x, 1 - b] + ky + (p_y1 - jnp.where(low, p0, roll_rows(p0, 1))))
            spread = (gx - g1) + (jnp.where(low, gy, roll_rows(gy, -1)) - g2) + (above_z(g3) - g3)
            dp = jnp.where(zmask, spread * winv[x, b], 0.0)
            dp_y = jnp.where(low, dp, roll_rows(dp, 1))
            keep = 1.0 - DAMP
            u1 = field(0, 0, 0, block)
            u2 = field(1, 0, 0, block)
            u3 = field(2, 0, 0, block)
            ux = field(0, 1, 0, block + a)
            uy = field(1, 0, 1, block)
            push = own_inv * dp
            slots[base + 0, block + 1] = jnp.where(zmask, keep * u1 + DAMP * (g1 + push), u1)
            slots[base + 1, block + 1] = jnp.where(zmask, keep * u2 + DAMP * (g2 + push), u2)
            slots[base + 2, block + 1] = jnp.where(
                z3, keep * u3 + DAMP * (g3 + own_inv * (dp - below_z(dp))), u3
            )
            slots[base + 3, block + 1] = p0 + DAMP * dp
            slots[base + 4, block + 1] = jnp.where(
                zmask & ymask, keep * uy + DAMP * (gy - inv_y * dp_y), uy
            )
            slots[base + 5, block + 1] = jnp.where(zmask, keep * ux + DAMP * (gx - inv_x * dp), ux)
            return carry

        lax.fori_loop(1, blocks + 1, block_step, 0)

        for k in range(NEW):
            send_x[side, 0, k] = slots[base + k, blocks + 1]
            send_x[side, 1, k] = slots[base + k, 2]
            for block in range(1, blocks + 1):
                send_y[side, 0, k, block - 1 : block] = slots[base + k, block + 1, 6:7]
                send_y[side, 1, k, block - 1 : block] = slots[base + k, block + 1, 1:2]
            for n in range(4):
                dx, dy = DIRECTIONS[4 + n]
                row = 6 if dy > 0 else 1
                send_c[side, n, k : k + 1] = slots[
                    base + k, blocks + 1 if dx > 0 else 2, row : row + 1
                ]

        def copy(n):
            if n < 2:
                src, dst = send_x.at[side, n], recv_x.at[side, n]
            elif n < 4:
                src, dst = send_y.at[side, n - 2], recv_y.at[side, n - 2]
            else:
                src, dst = send_c.at[side, n - 4], recv_c.at[side, n - 4]
            return pltpu.make_async_remote_copy(
                src_ref=src,
                dst_ref=dst,
                send_sem=send_sem.at[side, n],
                recv_sem=recv_sem.at[side, n],
                device_id=partner(n),
                device_id_type=MESH,
            )

        for n in (4, 5, 6, 7, 2, 3, 0, 1):
            guarded(present(n), lambda n=n: copy(n).start())
        for n in range(8):
            guarded(present(n), lambda n=n: copy(n).wait_send())
        for n in range(8):
            guarded(present(opposite(n)), lambda n=n: copy(n).wait_recv())

        has_low = lat > 0
        has_high = lat < lat_n - 1
        for k in range(NEW):
            for way, at, low_c, high_c in ((0, 1, 0, 1), (1, blocks + 2, 2, 3)):
                v = recv_x[side, way, k]
                v = jnp.where((rows == 0) & has_low, recv_c[side, low_c, k : k + 1], v)
                v = jnp.where((rows == 7) & has_high, recv_c[side, high_c, k : k + 1], v)
                slots[base + k, at] = v

        @pl.when(has_low)
        def _():
            for k in range(NEW):
                for block in range(1, blocks + 1):
                    slots[base + k, block + 1, 0:1] = recv_y[side, 0, k, block - 1 : block]

        @pl.when(has_high)
        def _():
            for k in range(NEW):
                for block in range(1, blocks + 1):
                    slots[base + k, block + 1, 7:8] = recv_y[side, 1, k, block - 1 : block]

        new = list(table)
        for xp in (0, 1):
            for yp in (0, 1):
                at = xp * 2 + yp
                same = (a == xp) & (b == yp)
                x_next = (a != xp) & (b == yp)
                y_next = (a == xp) & (b != yp)
                new[at] = jnp.where(same, base, jnp.where(x_next, base + 5, table[at]))
                new[16 + at] = jnp.where(same, 0, jnp.where(x_next, -a, table[16 + at]))
                new[4 + at] = jnp.where(same, base + 1, jnp.where(y_next, base + 4, table[4 + at]))
                new[8 + at] = jnp.where(same, base + 2, table[8 + at])
                new[12 + at] = jnp.where(same, base + 3, table[12 + at])
        return tuple(new)

    table = tuple(jnp.int32(n) for n in range(16)) + tuple(jnp.int32(0) for _ in range(4))
    table = lax.fori_loop(0, STEPS, sweep, table)

    def final(f, xp, yp, block):
        index = block + 1
        if f == 0:
            index = index + table[16 + xp * 2 + yp]
        return slots[table[f * 4 + xp * 2 + yp], index]

    def residual_sums(block, sums):
        sums = list(sums)
        for xp in (0, 1):
            for yp in (0, 1):
                x = 2 * block + xp

                def getter(f, xp=xp, yp=yp):
                    def get(dx, near):
                        at = block + (xp + dx) // 2
                        return final(f, (xp + dx) % 2, yp if near else 1 - yp, at)

                    return get

                ks = coupled(x, yp, [getter(0), getter(1), getter(2)])
                p0 = final(3, xp, yp, block)
                p_x = final(3, 1 - xp, yp, block - 1 + xp)
                p_y = final(3, xp, 1 - yp, block)
                if yp == 0:
                    p_y = roll_rows(p_y, 1)
                before = (p_x, p_y, below_z(p0))
                for d in range(3):
                    u = final(d, xp, yp, block)
                    mom = force[d, x, yp] - (diag[x, yp] * u - ks[d]) - (before[d] - p0)
                    sums[d] = sums[d] + mom
                sums[3] = sums[3] + vis[x, yp]
        return tuple(sums)

    odd_row = (rows & 1) == 1
    packed = []
    for part in range(2):
        zero = jnp.zeros(tile, jnp.float32)
        sums = lax.fori_loop(
            part * 4 + 1, part * 4 + 5, residual_sums, (zero, zero, zero, zero)
        )

        def collect(v):
            v = v + roll_rows(v, -1)
            v = v + roll_lanes(v, -1)
            return v + roll_lanes(v, -2)

        valid = odd_row & (rows < 7) & ((lanes & 3) == 0)
        below = jnp.where(valid, collect(sums[3]), 1.0)
        both = zero
        for d in range(3):
            value = jnp.where(valid, collect(sums[d]) / below, 0.0)
            both = both + (roll_lanes(value, d) if d else value)
        packed.append(both)
    own_part = packed[0] + roll_rows(packed[1], 1)
    shared[...] = own_part
    gathered[0] = own_part

    def spread_copy(hop):
        return pltpu.make_async_remote_copy(
            src_ref=shared,
            dst_ref=gathered.at[hop],
            send_sem=gsend_sem.at[hop],
            recv_sem=grecv_sem.at[hop],
            device_id=(lax.rem(lon + hop, lon_n), lat),
            device_id_type=MESH,
        )

    for hop in range(1, lon_n):
        spread_copy(hop).start()
    for hop in range(1, lon_n):
        spread_copy(hop).wait()

    cells = 2 * lon_n
    table_k = cycle_kernel(cells)
    smooth = []
    for part in range(2):
        total = jnp.zeros(tile, jnp.float32)
        for hop in range(lon_n):
            odd_k = table_k[(2 * hop + part) % cells]
            even_k = table_k[(2 * hop + part - 1) % cells]
            total = total + jnp.where(odd_row, odd_k, even_k) * gathered[hop]
        total = GAIN * (total + roll_rows(total, -1))
        per = []
        for d in range(3):
            v = jnp.where(odd_row & ((lanes & 3) == d), total, 0.0)
            if d:
                v = roll_lanes(v, -d)
            v = v + roll_lanes(v, 1)
            v = v + roll_lanes(v, 2)
            per.append(v + roll_rows(v, 1))
        smooth.append(per)

    for part in range(2):

        def finish(block, carry, part=part):
            for xp in (0, 1):
                for yp in (0, 1):
                    x = 2 * block + xp - 2
                    for d in range(3):
                        vel_out[d, x, yp] = final(d, xp, yp, block) + smooth[part][d]
                    own = vis[x + 2, yp]
                    p_out[x, yp] = final(3, xp, yp, block) / jnp.where(own > 0, own, 1.0)
            return carry

        lax.fori_loop(part * 4 + 1, part * 4 + 5, finish, 0)


def extended(block, sides, width):
    for axis, dim, periodic in sides:
        count = lax.axis_size(axis)
        forward = [(i, i + 1) for i in range(count - 1)]
        if periodic:
            forward.append((count - 1, 0))
        backward = [(target, source) for source, target in forward]
        low = lax.ppermute(
            lax.slice_in_dim(block, block.shape[dim] - width, None, axis=dim), axis, forward
        )
        high = lax.ppermute(lax.slice_in_dim(block, 0, width, axis=dim), axis, backward)
        block = jnp.concatenate([low, block, high], axis=dim)
    return block


def body(lon_n, lat_n, velocity, pressure_in, viscosity, body_force, colour_order):
    nx, ny, nz = viscosity.shape
    blocks = nx // 2
    stack = jnp.concatenate(
        [velocity, (pressure_in * viscosity)[None], body_force, viscosity[None]], axis=0
    )
    wide = extended(stack, (("lon", 1, True), ("lat", 2, False)), 2)
    wide = wide.reshape(8, nx + 4, 8, 2, nz).transpose(0, 1, 3, 2, 4)
    start = wide[:4].reshape(4, blocks + 2, 2, 2, 8, nz).transpose(0, 2, 3, 1, 4, 5)
    start = start.reshape(FIRST, blocks + 2, 8, nz)
    f32 = jnp.float32
    whole = pl.BlockSpec(memory_space=pltpu.VMEM)
    n_slots = FIRST + NEW * STEPS
    vel, pres = pl.pallas_call(
        functools.partial(kernel, lon_n, lat_n),
        out_shape=(
            jax.ShapeDtypeStruct((3, nx, 2, 8, nz), f32),
            jax.ShapeDtypeStruct((nx, 2, 8, nz), f32),
        ),
        in_specs=[
            pl.BlockSpec(memory_space=pltpu.SMEM),
            whole,
            whole,
            pl.BlockSpec(memory_space=pl.ANY),
        ],
        out_specs=(whole, whole),
        scratch_shapes=[
            pltpu.VMEM((n_slots, blocks + 3, 8, nz), f32),
            pltpu.VMEM((27, nx + 4, 2, 8, nz), f32),
            pltpu.VMEM((nx + 4, 2, 8, nz), f32),
            pltpu.VMEM((nx + 4, 2, 8, nz), f32),
            pltpu.VMEM((nx + 4, 2, 8, nz), f32),
            pltpu.VMEM((STEPS, 2, NEW, 8, nz), f32),
            pltpu.VMEM((STEPS, 2, NEW, 8, nz), f32),
            pltpu.VMEM((STEPS, 4, 8, nz), f32),
            pltpu.VMEM((STEPS, 2, NEW, 8, nz), f32),
            pltpu.VMEM((STEPS, 2, NEW, 8, nz), f32),
            pltpu.VMEM((STEPS, 4, 8, nz), f32),
            pltpu.VMEM((lon_n, 8, nz), f32),
            pltpu.VMEM((8, nz), f32),
            pltpu.SemaphoreType.DMA,
            pltpu.SemaphoreType.DMA((STEPS, 8)),
            pltpu.SemaphoreType.DMA((STEPS, 8)),
            pltpu.SemaphoreType.DMA((lon_n,)),
            pltpu.SemaphoreType.DMA((lon_n,)),
        ],
        compiler_params=pltpu.CompilerParams(
            collective_id=0, has_side_effects=True, vmem_limit_bytes=60 * 1024 * 1024
        ),
        name="vanka",
    )(colour_order, wide[7], wide[4:7], start)
    vel = vel[:, :, :, 1:7].transpose(0, 1, 3, 2, 4).reshape(3, nx, ny, nz)
    pres = pres[:, :, 1:7].transpose(0, 2, 1, 3).reshape(nx, ny, nz)
    return (vel, pres)


def solution(mesh):
    placed = (
        P(None, "lon", "lat", None),
        P("lon", "lat", None),
        P("lon", "lat", None),
        P(None, "lon", "lat", None),
        P(),
    )
    return jax.shard_map(
        functools.partial(body, mesh.shape["lon"], mesh.shape["lat"]),
        mesh=mesh,
        in_specs=placed,
        out_specs=(P(None, "lon", "lat", None), P("lon", "lat", None)),
        check_vma=False,
    )
```

```python
import functools
import math

import jax
import jax.numpy as jnp
from jax import lax
from jax.experimental import pallas as pl
from jax.experimental.pallas import tpu as pltpu
from jax.sharding import PartitionSpec as P

SWEEPS = 2
COLOURS = 8
STEPS = SWEEPS * COLOURS
DAMP = 0.6
GAIN = 0.25
NEW = 6
FIRST = 16
MESH = pl.DeviceIdType.MESH
DIRECTIONS = ((1, 0), (-1, 0), (0, 1), (0, -1), (1, 1), (1, -1), (-1, 1), (-1, -1))


def opposite(n):
    return DIRECTIONS.index((-DIRECTIONS[n][0], -DIRECTIONS[n][1]))


def kslot(dx, dy, dz):
    return ((dx + 1) * 3 + (dy + 1)) * 3 + (dz + 1)


def cycle_kernel(cells):
    rate = 4.0 / cells
    screening = 2.0 * math.cosh(rate) - 2.0
    factor = screening / (2.0 * math.sinh(rate) * math.sinh(rate * cells / 2.0))
    return [factor * math.cosh(rate * (cells / 2.0 - d)) for d in range(cells)]


def kernel(
    lon_n,
    lat_n,
    order_ref,
    vel_in,
    p_in,
    vis_in,
    force_in,
    vel_out,
    p_out,
    vis,
    force,
    slots,
    coup,
    diag,
    inv,
    winv,
    send_x,
    send_y,
    send_c,
    recv_x,
    recv_y,
    recv_c,
    gathered,
    shared,
    first_send_x,
    first_send_y,
    first_send_c,
    first_recv_x,
    first_recv_y,
    first_recv_c,
    first_send_sem,
    first_recv_sem,
    send_sem,
    recv_sem,
    gsend_sem,
    grecv_sem,
):
    lon = lax.axis_index("lon")
    lat = lax.axis_index("lat")
    planes = vis.shape[0]
    depth = vis.shape[-1]
    blocks = planes // 2 - 2
    tile = (8, depth)
    rows = lax.broadcasted_iota(jnp.int32, tile, 0)
    lanes = lax.broadcasted_iota(jnp.int32, tile, 1)

    def roll_rows(v, up):
        return pltpu.roll(v, up % 8, 0)

    def roll_lanes(v, up):
        return pltpu.roll(v, up % depth, 1)

    def above_z(v):
        return jnp.where(lanes == depth - 1, 0.0, roll_lanes(v, -1))

    def below_z(v):
        return jnp.where(lanes == 0, 0.0, roll_lanes(v, 1))

    def partner(n):
        dx, dy = DIRECTIONS[n]
        return (lax.rem(lon + dx + lon_n, lon_n), lat + dy)

    def present(n):
        dy = DIRECTIONS[n][1]
        if dy > 0:
            return lat < lat_n - 1
        if dy < 0:
            return lat > 0
        return None

    def guarded(cond, fn):
        if cond is None:
            fn()
        else:
            pl.when(cond)(fn)

    barrier = pltpu.get_barrier_semaphore()
    for n in range(8):

        def greet(n=n):
            pl.semaphore_signal(barrier, inc=1, device_id=partner(n), device_id_type=MESH)

        guarded(present(n), greet)
    for hop in range(2, lon_n - 1):
        pl.semaphore_signal(
            barrier, inc=1, device_id=(lax.rem(lon + hop, lon_n), lat), device_id_type=MESH
        )

    blank = jnp.zeros(tile, jnp.float32)

    def clear(x, carry):
        for yp in (0, 1):
            vis[x, yp] = blank
            for d in range(3):
                force[d, x, yp] = blank
        return carry

    lax.fori_loop(0, planes, clear, 0)

    def clear_slots(at, carry):
        for n in range(FIRST):
            slots[n, at] = blank
        return carry

    lax.fori_loop(0, blocks + 3, clear_slots, 0)

    def split(block, carry):
        for xp in (0, 1):
            x = 2 * block + xp - 2
            seen = vis_in[x]
            scaled = p_in[x] * seen
            for y in range(12):
                yp, row = y % 2, y // 2 + 1
                vis[x + 2, yp, row : row + 1] = seen[y : y + 1]
                slots[12 + xp * 2 + yp, block + 1, row : row + 1] = scaled[y : y + 1]
                for d in range(3):
                    slots[d * 4 + xp * 2 + yp, block + 1, row : row + 1] = vel_in[d, x, y : y + 1]
                    force[d, x + 2, yp, row : row + 1] = force_in[d, x, y : y + 1]
        return carry

    lax.fori_loop(1, blocks + 1, split, 0)

    def part(f, x, yp):
        if f == 7:
            return vis.at[x, yp]
        if f >= 4:
            return force.at[f - 4, x, yp]
        return slots.at[f * 4 + (x % 2) * 2 + yp, x // 2 + 1]

    first_x = (
        [(f, 1, yp) for f in (7, 0, 1, 2, 3) for yp in (0, 1)],
        [(f, planes - 2, yp) for f in (7, 4, 0, 1, 2, 3) for yp in (0, 1)]
        + [(f, planes - 1, yp) for f in (7, 0) for yp in (0, 1)],
    )
    first_y = (
        [(f, 0) for f in (7, 0, 1, 2, 3)] + [(f, 1) for f in (7, 0, 1, 2, 3, 4, 5, 6)],
        [(f, 0) for f in (7, 0, 1, 2, 3, 5)] + [(f, 1) for f in (7, 1)],
    )
    own_planes = planes - 4

    def first_copy(n):
        if n < 2:
            size = len(first_x[n])
            src = first_send_x.at[n, pl.ds(0, size)]
            dst = first_recv_x.at[n, pl.ds(0, size)]
        elif n < 4:
            size = len(first_y[n - 2])
            src = first_send_y.at[n - 2, pl.ds(0, size)]
            dst = first_recv_y.at[n - 2, pl.ds(0, size)]
        else:
            src, dst = first_send_c.at[n - 4], first_recv_c.at[n - 4]
        return pltpu.make_async_remote_copy(
            src_ref=src,
            dst_ref=dst,
            send_sem=first_send_sem.at[n],
            recv_sem=first_recv_sem.at[n],
            device_id=partner(n),
            device_id_type=MESH,
        )

    for way in (0, 1):
        for k, (f, x, yp) in enumerate(first_x[way]):
            source = part(f, x + own_planes if way == 0 else x - own_planes, yp)
            first_send_x[way, k] = source[...]
            for n in range(4):
                dx, dy = DIRECTIONS[4 + n]
                if (dx > 0) == (way == 0):
                    row = 6 if dy > 0 else 1
                    first_send_c[n, k : k + 1] = source[row : row + 1]
    ends = (lat == 0).astype(jnp.int32) + (lat == lat_n - 1).astype(jnp.int32)
    pl.semaphore_wait(barrier, lon_n + 5 - 3 * ends)
    for n in (4, 5, 6, 7, 0, 1):
        guarded(present(n), lambda n=n: first_copy(n).start())
    for way in (0, 1):
        row = 6 if way == 0 else 1
        for k, (f, yp) in enumerate(first_y[way]):
            for x in range(own_planes):
                first_send_y[way, k, x : x + 1] = part(f, x + 2, yp)[row : row + 1]
        guarded(present(2 + way), lambda n=2 + way: first_copy(n).start())
    for n in range(8):
        guarded(present(opposite(n)), lambda n=n: first_copy(n).wait_recv())
    has_low = lat > 0
    has_high = lat < lat_n - 1
    for way in (0, 1):
        low_c, high_c = (0, 1) if way == 0 else (2, 3)
        for k, (f, x, yp) in enumerate(first_x[way]):
            v = first_recv_x[way, k]
            v = jnp.where((rows == 0) & has_low, first_recv_c[low_c, k : k + 1], v)
            v = jnp.where((rows == 7) & has_high, first_recv_c[high_c, k : k + 1], v)
            part(f, x, yp)[...] = v

    def first_rows(way, row):
        for k, (f, yp) in enumerate(first_y[way]):
            for x in range(own_planes):
                part(f, x + 2, yp)[row : row + 1] = first_recv_y[way, k, x : x + 1]

    pl.when(has_low)(lambda: first_rows(0, 0))
    pl.when(has_high)(lambda: first_rows(1, 7))

    def inside(yp):
        y = lat * 12 + 2 * (rows - 1) + yp
        return (y >= 0) & (y < 12 * lat_n)

    half = [(1, dy, dz) for dy in (-1, 0, 1) for dz in (-1, 0, 1)]
    half += [(0, 1, dz) for dz in (-1, 0, 1)] + [(0, 0, 1)]

    def couple(x, carry):
        for yp in (0, 1):
            own = vis[x, yp]
            for dx in (0, 1):
                for dy in (-1, 0, 1):
                    offsets = [o for o in half if o[0] == dx and o[1] == dy]
                    if not offsets:
                        continue
                    other_yp = yp if dy == 0 else 1 - yp
                    shift = 0
                    if dy == 1 and yp == 1:
                        shift = -1
                    if dy == -1 and yp == 0:
                        shift = 1
                    other = vis[x + dx, other_yp]
                    if shift:
                        other = roll_rows(other, shift)
                    for o in offsets:
                        dz = o[2]
                        beside = other
                        if dz == 1:
                            beside = above_z(other)
                        elif dz == -1:
                            beside = below_z(other)
                        reach = abs(dx) + abs(dy) + abs(dz)
                        scale = 2.0 * 0.5 ** (reach - 1)
                        value = (scale * own) * beside / jnp.maximum(own + beside, 1.0)
                        coup[kslot(*o), x, yp] = value
                        back = value
                        if dz:
                            back = roll_lanes(back, dz)
                        if shift:
                            back = roll_rows(back, -shift)
                        coup[kslot(-dx, -dy, -dz), x + dx, other_yp] = back
        return carry

    lax.fori_loop(1, planes - 1, couple, 0)

    def diagonal(x, carry):
        for yp in (0, 1):
            total = jnp.zeros(tile, jnp.float32)
            for n in range(27):
                if n != 13:
                    total = total + coup[n, x, yp]
            diag[x, yp] = total
            ok = inside(yp) & (total > 0)
            inv[x, yp] = jnp.where(ok, 1.0 / jnp.where(ok, total, 1.0), 0.0)
        return carry

    lax.fori_loop(2, planes - 1, diagonal, 0)

    def weights(x, carry):
        for yp in (0, 1):
            own = inv[x, yp]
            up = inv[x, 1 - yp]
            if yp == 1:
                up = roll_rows(up, -1)
            total = 3.0 * own + inv[x + 1, yp] + up + above_z(own)
            ok = inside(yp) & (total > 0)
            winv[x, yp] = jnp.where(ok, 1.0 / jnp.where(ok, total, 1.0), 0.0)
        return carry

    lax.fori_loop(2, planes - 2, weights, 0)

    def coupled(x, t, fields):
        at_low = t == 0

        def turn(v):
            return jnp.where(at_low, roll_rows(v, 1), roll_rows(v, -1))

        sums = [[None] * 3 for _ in fields]

        def gather(dy, yp, near):
            for dx in (-1, 0, 1):
                tiles = [f(dx, near) for f in fields]
                for dz in (-1, 0, 1):
                    if near and dx == 0 and dz == 0:
                        continue
                    k = coup[((1 - dx) * 3 + (1 - dy)) * 3 + (1 - dz), x + dx, yp]
                    for n, v in enumerate(tiles):
                        term = k * v
                        old = sums[n][dz + 1]
                        sums[n][dz + 1] = term if old is None else old + term

        gather(jnp.where(at_low, -1, 1), 1 - t, 0)
        for n in range(len(fields)):
            sums[n] = [turn(v) for v in sums[n]]
        gather(jnp.where(at_low, 1, -1), 1 - t, 0)
        gather(0, t, 1)
        return [s[1] + roll_lanes(s[2], -1) + roll_lanes(s[0], 1) for s in sums]

    def pick(table, xp, yp):
        low = jnp.where(yp == 0, table[0], table[1])
        high = jnp.where(yp == 0, table[2], table[3])
        return jnp.where(xp == 0, low, high)

    def copy(n, side):
        if n < 2:
            src, dst = send_x.at[side, n], recv_x.at[side, n]
        elif n < 4:
            src, dst = send_y.at[side, n - 2], recv_y.at[side, n - 2]
        else:
            src, dst = send_c.at[side, n - 4], recv_c.at[side, n - 4]
        return pltpu.make_async_remote_copy(
            src_ref=src,
            dst_ref=dst,
            send_sem=send_sem.at[side, n],
            recv_sem=recv_sem.at[side, n],
            device_id=partner(n),
            device_id_type=MESH,
        )

    def sweep(s, table):
        colour = order_ref[lax.rem(s, COLOURS)]
        a = colour & 1
        b = (colour >> 1) & 1
        c = (colour >> 2) & 1
        base = FIRST + NEW * s
        side = s
        rel = {}
        for f in range(4):
            for xr in (0, 1):
                for yr in (0, 1):
                    rel[f, xr, yr] = pick(table[f * 4 : f * 4 + 4], a ^ xr, b ^ yr)
        shift = {
            (xr, yr): pick(table[16:20], a ^ xr, b ^ yr) for xr in (0, 1) for yr in (0, 1)
        }

        def field(f, xr, yr, block):
            index = block + 1
            if f == 0:
                index = index + shift[xr, yr]
            return slots[rel[f, xr, yr], index]

        zmask = (lanes & 1) == c
        z3 = (lanes > 0) | (c == 0)
        ymask = lat * 12 + 2 * (rows - 1) + (1 - b) >= 1
        low = b == 0

        def block_step(block, carry):
            x = 2 * block + a

            def main(f):
                def get(dx, near):
                    at = block if dx == 0 else (block - 1 + a if dx < 0 else block + a)
                    return field(f, abs(dx), 0 if near else 1, at)

                return get

            def xprime(dx, near):
                at = block + a if dx == 0 else (block if dx < 0 else block + 1)
                return field(0, 1 - abs(dx), 0 if near else 1, at)

            def yprime(dx, near):
                at = block if dx == 0 else (block - 1 + a if dx < 0 else block + a)
                return field(1, abs(dx), 1 if near else 0, at)

            p0 = field(3, 0, 0, block)
            p_x = field(3, 1, 0, block - 1 + a)
            p_x1 = field(3, 1, 0, block + a)
            p_y1 = field(3, 0, 1, block)
            k1, k2, k3 = coupled(x, b, [main(0), main(1), main(2)])
            own_inv = inv[x, b]
            p_y = jnp.where(low, roll_rows(p_y1, 1), p_y1)
            g1 = own_inv * (force[0, x, b] + k1 + (p0 - p_x))
            g2 = own_inv * (force[1, x, b] + k2 + (p0 - p_y))
            g3 = own_inv * (force[2, x, b] + k3 + (p0 - below_z(p0)))
            (kx,) = coupled(x + 1, b, [xprime])
            inv_x = inv[x + 1, b]
            gx = inv_x * (force[0, x + 1, b] + kx + (p_x1 - p0))
            (ky,) = coupled(x, 1 - b, [yprime])
            inv_y = inv[x, 1 - b]
            gy = inv_y * (force[1, x, 1 - b] + ky + (p_y1 - jnp.where(low, p0, roll_rows(p0, 1))))
            spread = (gx - g1) + (jnp.where(low, gy, roll_rows(gy, -1)) - g2) + (above_z(g3) - g3)
            dp = jnp.where(zmask, spread * winv[x, b], 0.0)
            dp_y = jnp.where(low, dp, roll_rows(dp, 1))
            keep = 1.0 - DAMP
            u1 = field(0, 0, 0, block)
            u2 = field(1, 0, 0, block)
            u3 = field(2, 0, 0, block)
            ux = field(0, 1, 0, block + a)
            uy = field(1, 0, 1, block)
            push = own_inv * dp
            slots[base + 0, block + 1] = jnp.where(zmask, keep * u1 + DAMP * (g1 + push), u1)
            slots[base + 1, block + 1] = jnp.where(zmask, keep * u2 + DAMP * (g2 + push), u2)
            slots[base + 2, block + 1] = jnp.where(
                z3, keep * u3 + DAMP * (g3 + own_inv * (dp - below_z(dp))), u3
            )
            slots[base + 3, block + 1] = p0 + DAMP * dp
            slots[base + 4, block + 1] = jnp.where(
                zmask & ymask, keep * uy + DAMP * (gy - inv_y * dp_y), uy
            )
            slots[base + 5, block + 1] = jnp.where(zmask, keep * ux + DAMP * (gx - inv_x * dp), ux)
            return carry

        lax.fori_loop(0, 2, lambda n, t: block_step(1 + n * (blocks - 1), t), 0)
        for k in range(NEW):
            send_x[side, 0, k] = slots[base + k, blocks + 1]
            send_x[side, 1, k] = slots[base + k, 2]
            for n in range(4):
                dx, dy = DIRECTIONS[4 + n]
                row = 6 if dy > 0 else 1
                send_c[side, n, k : k + 1] = slots[
                    base + k, blocks + 1 if dx > 0 else 2, row : row + 1
                ]
        for n in (4, 5, 6, 7, 0, 1):
            guarded(present(n), lambda n=n: copy(n, side).start())
        lax.fori_loop(2, blocks, block_step, 0, unroll=2)
        for k in range(NEW):
            for block in range(1, blocks + 1):
                send_y[side, 0, k, block - 1 : block] = slots[base + k, block + 1, 6:7]
                send_y[side, 1, k, block - 1 : block] = slots[base + k, block + 1, 1:2]
        for n in (2, 3):
            guarded(present(n), lambda n=n: copy(n, side).start())
        for n in range(8):
            guarded(present(opposite(n)), lambda n=n: copy(n, side).wait_recv())

        for k in range(NEW):
            for way, at, low_c, high_c in ((0, 1, 0, 1), (1, blocks + 2, 2, 3)):
                v = recv_x[side, way, k]
                v = jnp.where((rows == 0) & has_low, recv_c[side, low_c, k : k + 1], v)
                v = jnp.where((rows == 7) & has_high, recv_c[side, high_c, k : k + 1], v)
                slots[base + k, at] = v

        @pl.when(has_low)
        def _():
            for k in range(NEW):
                for block in range(1, blocks + 1):
                    slots[base + k, block + 1, 0:1] = recv_y[side, 0, k, block - 1 : block]

        @pl.when(has_high)
        def _():
            for k in range(NEW):
                for block in range(1, blocks + 1):
                    slots[base + k, block + 1, 7:8] = recv_y[side, 1, k, block - 1 : block]

        new = list(table)
        for xp in (0, 1):
            for yp in (0, 1):
                at = xp * 2 + yp
                same = (a == xp) & (b == yp)
                x_next = (a != xp) & (b == yp)
                y_next = (a == xp) & (b != yp)
                new[at] = jnp.where(same, base, jnp.where(x_next, base + 5, table[at]))
                new[16 + at] = jnp.where(same, 0, jnp.where(x_next, -a, table[16 + at]))
                new[4 + at] = jnp.where(same, base + 1, jnp.where(y_next, base + 4, table[4 + at]))
                new[8 + at] = jnp.where(same, base + 2, table[8 + at])
                new[12 + at] = jnp.where(same, base + 3, table[12 + at])
        return tuple(new)

    table = tuple(jnp.int32(n) for n in range(16)) + tuple(jnp.int32(0) for _ in range(4))
    table = lax.fori_loop(0, STEPS, sweep, table)

    def final(f, xp, yp, block):
        index = block + 1
        if f == 0:
            index = index + table[16 + xp * 2 + yp]
        return slots[table[f * 4 + xp * 2 + yp], index]

    def residual_sums(block, sums):
        sums = list(sums)
        for xp in (0, 1):
            for yp in (0, 1):
                x = 2 * block + xp

                def getter(f, xp=xp, yp=yp):
                    def get(dx, near):
                        at = block + (xp + dx) // 2
                        return final(f, (xp + dx) % 2, yp if near else 1 - yp, at)

                    return get

                ks = coupled(x, yp, [getter(0), getter(1), getter(2)])
                p0 = final(3, xp, yp, block)
                p_x = final(3, 1 - xp, yp, block - 1 + xp)
                p_y = final(3, xp, 1 - yp, block)
                if yp == 0:
                    p_y = roll_rows(p_y, 1)
                before = (p_x, p_y, below_z(p0))
                for d in range(3):
                    u = final(d, xp, yp, block)
                    mom = force[d, x, yp] - (diag[x, yp] * u - ks[d]) - (before[d] - p0)
                    sums[d] = sums[d] + mom
                sums[3] = sums[3] + vis[x, yp]
        return tuple(sums)

    odd_row = (rows & 1) == 1
    packed = []
    for half_no in range(2):
        zero = jnp.zeros(tile, jnp.float32)
        sums = lax.fori_loop(
            half_no * 4 + 1, half_no * 4 + 5, residual_sums, (zero, zero, zero, zero)
        )

        def collect(v):
            v = v + roll_rows(v, -1)
            v = v + roll_lanes(v, -1)
            return v + roll_lanes(v, -2)

        valid = odd_row & (rows < 7) & ((lanes & 3) == 0)
        below = jnp.where(valid, collect(sums[3]), 1.0)
        both = zero
        for d in range(3):
            value = jnp.where(valid, collect(sums[d]) / below, 0.0)
            both = both + (roll_lanes(value, d) if d else value)
        packed.append(both)
    own_part = packed[0] + roll_rows(packed[1], 1)
    shared[...] = own_part
    gathered[0] = own_part

    def spread_copy(hop):
        return pltpu.make_async_remote_copy(
            src_ref=shared,
            dst_ref=gathered.at[hop],
            send_sem=gsend_sem.at[hop],
            recv_sem=grecv_sem.at[hop],
            device_id=(lax.rem(lon + hop, lon_n), lat),
            device_id_type=MESH,
        )

    for hop in range(1, lon_n):
        spread_copy(hop).start()
    for hop in range(1, lon_n):
        spread_copy(hop).wait()

    for n in range(8):
        guarded(present(n), lambda n=n: first_copy(n).wait_send())

    def drain(s, carry):
        for n in range(8):
            guarded(present(n), lambda n=n: copy(n, s).wait_send())
        return carry

    lax.fori_loop(0, STEPS, drain, 0)

    cells = 2 * lon_n
    table_k = cycle_kernel(cells)
    smooth = []
    for half_no in range(2):
        total = jnp.zeros(tile, jnp.float32)
        for hop in range(lon_n):
            odd_k = table_k[(2 * hop + half_no) % cells]
            even_k = table_k[(2 * hop + half_no - 1) % cells]
            total = total + jnp.where(odd_row, odd_k, even_k) * gathered[hop]
        total = GAIN * (total + roll_rows(total, -1))
        per = []
        for d in range(3):
            v = jnp.where(odd_row & ((lanes & 3) == d), total, 0.0)
            if d:
                v = roll_lanes(v, -d)
            v = v + roll_lanes(v, 1)
            v = v + roll_lanes(v, 2)
            per.append(v + roll_rows(v, 1))
        smooth.append(per)

    for half_no in range(2):

        def finish(block, carry, half_no=half_no):
            for xp in (0, 1):
                for yp in (0, 1):
                    x = 2 * block + xp - 2
                    for d in range(3):
                        v = final(d, xp, yp, block) + smooth[half_no][d]
                        for row in range(6):
                            y = 2 * row + yp
                            vel_out[d, x, y : y + 1] = v[row + 1 : row + 2]
                    own = vis[x + 2, yp]
                    v = final(3, xp, yp, block) / jnp.where(own > 0, own, 1.0)
                    for row in range(6):
                        y = 2 * row + yp
                        p_out[x, y : y + 1] = v[row + 1 : row + 2]
            return carry

        lax.fori_loop(half_no * 4 + 1, half_no * 4 + 5, finish, 0)


def body(lon_n, lat_n, velocity, pressure_in, viscosity, body_force, colour_order):
    nx, ny, nz = viscosity.shape
    blocks = nx // 2
    f32 = jnp.float32
    whole = pl.BlockSpec(memory_space=pltpu.VMEM)
    n_slots = FIRST + NEW * STEPS
    return pl.pallas_call(
        functools.partial(kernel, lon_n, lat_n),
        out_shape=(
            jax.ShapeDtypeStruct((3, nx, ny, nz), f32),
            jax.ShapeDtypeStruct((nx, ny, nz), f32),
        ),
        in_specs=[pl.BlockSpec(memory_space=pltpu.SMEM)] + [whole] * 4,
        out_specs=(whole, whole),
        scratch_shapes=[
            pltpu.VMEM((nx + 4, 2, 8, nz), f32),
            pltpu.VMEM((3, nx + 4, 2, 8, nz), f32),
            pltpu.VMEM((n_slots, blocks + 3, 8, nz), f32),
            pltpu.VMEM((27, nx + 4, 2, 8, nz), f32),
            pltpu.VMEM((nx + 4, 2, 8, nz), f32),
            pltpu.VMEM((nx + 4, 2, 8, nz), f32),
            pltpu.VMEM((nx + 4, 2, 8, nz), f32),
            pltpu.VMEM((STEPS, 2, NEW, 8, nz), f32),
            pltpu.VMEM((STEPS, 2, NEW, 8, nz), f32),
            pltpu.VMEM((STEPS, 4, 8, nz), f32),
            pltpu.VMEM((STEPS, 2, NEW, 8, nz), f32),
            pltpu.VMEM((STEPS, 2, NEW, 8, nz), f32),
            pltpu.VMEM((STEPS, 4, 8, nz), f32),
            pltpu.VMEM((lon_n, 8, nz), f32),
            pltpu.VMEM((8, nz), f32),
            pltpu.VMEM((2, 16, 8, nz), f32),
            pltpu.VMEM((2, 13, nx, nz), f32),
            pltpu.VMEM((4, 16, nz), f32),
            pltpu.VMEM((2, 16, 8, nz), f32),
            pltpu.VMEM((2, 13, nx, nz), f32),
            pltpu.VMEM((4, 16, nz), f32),
            pltpu.SemaphoreType.DMA((8,)),
            pltpu.SemaphoreType.DMA((8,)),
            pltpu.SemaphoreType.DMA((STEPS, 8)),
            pltpu.SemaphoreType.DMA((STEPS, 8)),
            pltpu.SemaphoreType.DMA((lon_n,)),
            pltpu.SemaphoreType.DMA((lon_n,)),
        ],
        compiler_params=pltpu.CompilerParams(
            collective_id=0, has_side_effects=True, vmem_limit_bytes=60 * 1024 * 1024
        ),
        name="vanka",
    )(colour_order, velocity, pressure_in, viscosity, body_force)


def solution(mesh):
    placed = (
        P(None, "lon", "lat", None),
        P("lon", "lat", None),
        P("lon", "lat", None),
        P(None, "lon", "lat", None),
        P(),
    )
    return jax.shard_map(
        functools.partial(body, mesh.shape["lon"], mesh.shape["lat"]),
        mesh=mesh,
        in_specs=placed,
        out_specs=(P(None, "lon", "lat", None), P("lon", "lat", None)),
        check_vma=False,
    )
```

```python
import functools
import math

import jax
import jax.numpy as jnp
from jax import lax
from jax.experimental import pallas as pl
from jax.experimental.pallas import tpu as pltpu
from jax.sharding import PartitionSpec as P

SWEEPS = 2
COLOURS = 8
STEPS = SWEEPS * COLOURS
DAMP = 0.6
GAIN = 0.25
SENT = 4
NEW = 6
FIRST = 16
MESH = pl.DeviceIdType.MESH
DIRECTIONS = ((1, 0), (-1, 0), (0, 1), (0, -1), (1, 1), (1, -1), (-1, 1), (-1, -1))


def opposite(n):
    return DIRECTIONS.index((-DIRECTIONS[n][0], -DIRECTIONS[n][1]))


def kslot(dx, dy, dz):
    return ((dx + 1) * 3 + (dy + 1)) * 3 + (dz + 1)


def cycle_kernel(cells):
    rate = 4.0 / cells
    screening = 2.0 * math.cosh(rate) - 2.0
    factor = screening / (2.0 * math.sinh(rate) * math.sinh(rate * cells / 2.0))
    return [factor * math.cosh(rate * (cells / 2.0 - d)) for d in range(cells)]


def kernel(
    lon_n,
    lat_n,
    order_ref,
    vel_hbm,
    p_hbm,
    vis_hbm,
    force_hbm,
    vel_out,
    p_out,
    vel_in,
    p_in,
    vis_in,
    force_in,
    vis,
    force,
    slots,
    coup,
    diag,
    inv,
    winv,
    send_x,
    send_y,
    send_c,
    recv_x,
    recv_y,
    recv_c,
    gathered,
    shared,
    first_send_x,
    first_send_y,
    first_send_c,
    first_recv_x,
    first_recv_y,
    first_recv_c,
    first_send_sem,
    first_recv_sem,
    pack,
    load_sem,
    send_sem,
    recv_sem,
    gsend_sem,
    grecv_sem,
):
    lon = lax.axis_index("lon")
    lat = lax.axis_index("lat")
    planes = vis.shape[0]
    depth = vis.shape[-1]
    blocks = planes // 2 - 2
    tile = (8, depth)
    rows = lax.broadcasted_iota(jnp.int32, tile, 0)
    lanes = lax.broadcasted_iota(jnp.int32, tile, 1)

    def roll_rows(v, up):
        return pltpu.roll(v, up % 8, 0)

    def roll_lanes(v, up):
        return pltpu.roll(v, up % depth, 1)

    def above_z(v):
        return jnp.where(lanes == depth - 1, 0.0, roll_lanes(v, -1))

    def below_z(v):
        return jnp.where(lanes == 0, 0.0, roll_lanes(v, 1))

    def partner(n):
        dx, dy = DIRECTIONS[n]
        return (lax.rem(lon + dx + lon_n, lon_n), lat + dy)

    def present(n):
        dy = DIRECTIONS[n][1]
        if dy > 0:
            return lat < lat_n - 1
        if dy < 0:
            return lat > 0
        return None

    def guarded(cond, fn):
        if cond is None:
            fn()
        else:
            pl.when(cond)(fn)

    pairs = ((vis_hbm, vis_in), (p_hbm, p_in), (vel_hbm, vel_in), (force_hbm, force_in))
    loads = [pltpu.make_async_copy(src, dst, load_sem.at[n]) for n, (src, dst) in enumerate(pairs)]
    for copy_in in loads:
        copy_in.start()

    barrier = pltpu.get_barrier_semaphore()
    for n in range(8):

        def greet(n=n):
            pl.semaphore_signal(barrier, inc=1, device_id=partner(n), device_id_type=MESH)

        guarded(present(n), greet)
    for hop in range(2, lon_n - 1):
        pl.semaphore_signal(
            barrier, inc=1, device_id=(lax.rem(lon + hop, lon_n), lat), device_id_type=MESH
        )

    blank = jnp.zeros(tile, jnp.float32)

    def clear(x, carry):
        for yp in (0, 1):
            vis[x, yp] = blank
            for d in range(3):
                force[d, x, yp] = blank
        return carry

    lax.fori_loop(0, planes, clear, 0)

    def clear_slots(at, carry):
        for n in range(FIRST):
            slots[n, at] = blank
        return carry

    lax.fori_loop(0, blocks + 3, clear_slots, 0)

    def split(block, carry):
        for xp in (0, 1):
            x = 2 * block + xp - 2
            seen = vis_in[x]
            scaled = p_in[x] * seen
            for y in range(12):
                yp, row = y % 2, y // 2 + 1
                vis[x + 2, yp, row : row + 1] = seen[y : y + 1]
                slots[12 + xp * 2 + yp, block + 1, row : row + 1] = scaled[y : y + 1]
                for d in range(3):
                    slots[d * 4 + xp * 2 + yp, block + 1, row : row + 1] = vel_in[d, x, y : y + 1]
                    force[d, x + 2, yp, row : row + 1] = force_in[d, x, y : y + 1]
        return carry

    for copy_in in loads:
        copy_in.wait()
    lax.fori_loop(1, blocks + 1, split, 0)

    def part(f, x, yp):
        if f == 7:
            return vis.at[x, yp]
        if f >= 4:
            return force.at[f - 4, x, yp]
        return slots.at[f * 4 + (x % 2) * 2 + yp, x // 2 + 1]

    first_x = (
        [(f, 1, yp) for f in (7, 0, 1, 2, 3) for yp in (0, 1)],
        [(f, planes - 2, yp) for f in (7, 4, 0, 1, 2, 3) for yp in (0, 1)]
        + [(f, planes - 1, yp) for f in (7, 0) for yp in (0, 1)],
    )
    first_y = (
        [(f, 0) for f in (7, 0, 1, 2, 3)] + [(f, 1) for f in (7, 0, 1, 2, 3, 4, 5, 6)],
        [(f, 0) for f in (7, 0, 1, 2, 3, 5)] + [(f, 1) for f in (7, 1)],
    )
    own_planes = planes - 4

    def first_copy(n):
        if n < 2:
            size = len(first_x[n])
            src = first_send_x.at[n, pl.ds(0, size)]
            dst = first_recv_x.at[n, pl.ds(0, size)]
        elif n < 4:
            size = len(first_y[n - 2])
            src = first_send_y.at[n - 2, pl.ds(0, size)]
            dst = first_recv_y.at[n - 2, pl.ds(0, size)]
        else:
            src, dst = first_send_c.at[n - 4], first_recv_c.at[n - 4]
        return pltpu.make_async_remote_copy(
            src_ref=src,
            dst_ref=dst,
            send_sem=first_send_sem.at[n],
            recv_sem=first_recv_sem.at[n],
            device_id=partner(n),
            device_id_type=MESH,
        )

    for way in (0, 1):
        for k, (f, x, yp) in enumerate(first_x[way]):
            source = part(f, x + own_planes if way == 0 else x - own_planes, yp)
            first_send_x[way, k] = source[...]
            for n in range(4):
                dx, dy = DIRECTIONS[4 + n]
                if (dx > 0) == (way == 0):
                    row = 6 if dy > 0 else 1
                    first_send_c[n, k : k + 1] = source[row : row + 1]
    ends = (lat == 0).astype(jnp.int32) + (lat == lat_n - 1).astype(jnp.int32)
    pl.semaphore_wait(barrier, lon_n + 5 - 3 * ends)
    for n in (4, 5, 6, 7, 0, 1):
        guarded(present(n), lambda n=n: first_copy(n).start())
    for way in (0, 1):
        row = 6 if way == 0 else 1
        for k, (f, yp) in enumerate(first_y[way]):
            for x in range(own_planes):
                first_send_y[way, k, x : x + 1] = part(f, x + 2, yp)[row : row + 1]
        guarded(present(2 + way), lambda n=2 + way: first_copy(n).start())
    for n in range(8):
        guarded(present(opposite(n)), lambda n=n: first_copy(n).wait_recv())
    has_low = lat > 0
    has_high = lat < lat_n - 1
    for way in (0, 1):
        low_c, high_c = (0, 1) if way == 0 else (2, 3)
        for k, (f, x, yp) in enumerate(first_x[way]):
            v = first_recv_x[way, k]
            v = jnp.where((rows == 0) & has_low, first_recv_c[low_c, k : k + 1], v)
            v = jnp.where((rows == 7) & has_high, first_recv_c[high_c, k : k + 1], v)
            part(f, x, yp)[...] = v

    def first_rows(way, row):
        for k, (f, yp) in enumerate(first_y[way]):
            for x in range(own_planes):
                part(f, x + 2, yp)[row : row + 1] = first_recv_y[way, k, x : x + 1]

    pl.when(has_low)(lambda: first_rows(0, 0))
    pl.when(has_high)(lambda: first_rows(1, 7))

    def inside(yp):
        y = lat * 12 + 2 * (rows - 1) + yp
        return (y >= 0) & (y < 12 * lat_n)

    half = [(1, dy, dz) for dy in (-1, 0, 1) for dz in (-1, 0, 1)]
    half += [(0, 1, dz) for dz in (-1, 0, 1)] + [(0, 0, 1)]

    def couple(x, carry):
        for yp in (0, 1):
            own = vis[x, yp]
            for dx in (0, 1):
                for dy in (-1, 0, 1):
                    offsets = [o for o in half if o[0] == dx and o[1] == dy]
                    if not offsets:
                        continue
                    other_yp = yp if dy == 0 else 1 - yp
                    shift = 0
                    if dy == 1 and yp == 1:
                        shift = -1
                    if dy == -1 and yp == 0:
                        shift = 1
                    other = vis[x + dx, other_yp]
                    if shift:
                        other = roll_rows(other, shift)
                    for o in offsets:
                        dz = o[2]
                        beside = other
                        if dz == 1:
                            beside = above_z(other)
                        elif dz == -1:
                            beside = below_z(other)
                        reach = abs(dx) + abs(dy) + abs(dz)
                        scale = 2.0 * 0.5 ** (reach - 1)
                        value = (scale * own) * beside / jnp.maximum(own + beside, 1.0)
                        coup[kslot(*o), x, yp] = value
                        back = value
                        if dz:
                            back = roll_lanes(back, dz)
                        if shift:
                            back = roll_rows(back, -shift)
                        coup[kslot(-dx, -dy, -dz), x + dx, other_yp] = back
        return carry

    lax.fori_loop(1, planes - 1, couple, 0)

    def diagonal(x, carry):
        for yp in (0, 1):
            total = jnp.zeros(tile, jnp.float32)
            for n in range(27):
                if n != 13:
                    total = total + coup[n, x, yp]
            diag[x, yp] = total
            ok = inside(yp) & (total > 0)
            inv[x, yp] = jnp.where(ok, 1.0 / jnp.where(ok, total, 1.0), 0.0)
        return carry

    lax.fori_loop(2, planes - 1, diagonal, 0)

    def weights(x, carry):
        for yp in (0, 1):
            own = inv[x, yp]
            up = inv[x, 1 - yp]
            if yp == 1:
                up = roll_rows(up, -1)
            total = 3.0 * own + inv[x + 1, yp] + up + above_z(own)
            ok = inside(yp) & (total > 0)
            winv[x, yp] = jnp.where(ok, 1.0 / jnp.where(ok, total, 1.0), 0.0)
        return carry

    lax.fori_loop(2, planes - 2, weights, 0)

    def coupled(x, t, fields):
        at_low = t == 0

        def turn(v):
            return jnp.where(at_low, roll_rows(v, 1), roll_rows(v, -1))

        sums = [[None] * 3 for _ in fields]

        def gather(dy, yp, near):
            for dx in (-1, 0, 1):
                tiles = [f(dx, near) for f in fields]
                for dz in (-1, 0, 1):
                    if near and dx == 0 and dz == 0:
                        continue
                    k = coup[((1 - dx) * 3 + (1 - dy)) * 3 + (1 - dz), x + dx, yp]
                    for n, v in enumerate(tiles):
                        term = k * v
                        old = sums[n][dz + 1]
                        sums[n][dz + 1] = term if old is None else old + term

        gather(jnp.where(at_low, -1, 1), 1 - t, 0)
        for n in range(len(fields)):
            sums[n] = [turn(v) for v in sums[n]]
        gather(jnp.where(at_low, 1, -1), 1 - t, 0)
        gather(0, t, 1)
        return [s[1] + roll_lanes(s[2], -1) + roll_lanes(s[0], 1) for s in sums]

    def pick(table, xp, yp):
        low = jnp.where(yp == 0, table[0], table[1])
        high = jnp.where(yp == 0, table[2], table[3])
        return jnp.where(xp == 0, low, high)

    def copy(n, side):
        if n < 2:
            src, dst = send_x.at[side, n], recv_x.at[side, n]
        elif n < 4:
            src, dst = send_y.at[side, n - 2], recv_y.at[side, n - 2]
        else:
            src, dst = send_c.at[side, n - 4], recv_c.at[side, n - 4]
        return pltpu.make_async_remote_copy(
            src_ref=src,
            dst_ref=dst,
            send_sem=send_sem.at[side, n],
            recv_sem=recv_sem.at[side, n],
            device_id=partner(n),
            device_id_type=MESH,
        )

    def sweep(s, table):
        colour = order_ref[lax.rem(s, COLOURS)]
        a = colour & 1
        b = (colour >> 1) & 1
        c = (colour >> 2) & 1
        base = FIRST + NEW * s
        side = s
        rel = {}
        for f in range(4):
            for xr in (0, 1):
                for yr in (0, 1):
                    rel[f, xr, yr] = pick(table[f * 4 : f * 4 + 4], a ^ xr, b ^ yr)
        shift = {
            (xr, yr): pick(table[16:20], a ^ xr, b ^ yr) for xr in (0, 1) for yr in (0, 1)
        }

        def field(f, xr, yr, block):
            index = block + 1
            if f == 0:
                index = index + shift[xr, yr]
            return slots[rel[f, xr, yr], index]

        zmask = (lanes & 1) == c
        z3 = (lanes > 0) | (c == 0)
        ymask = lat * 12 + 2 * (rows - 1) + (1 - b) >= 1
        low = b == 0

        def block_step(block, carry):
            x = 2 * block + a

            def main(f):
                def get(dx, near):
                    at = block if dx == 0 else (block - 1 + a if dx < 0 else block + a)
                    return field(f, abs(dx), 0 if near else 1, at)

                return get

            def xprime(dx, near):
                at = block + a if dx == 0 else (block if dx < 0 else block + 1)
                return field(0, 1 - abs(dx), 0 if near else 1, at)

            def yprime(dx, near):
                at = block if dx == 0 else (block - 1 + a if dx < 0 else block + a)
                return field(1, abs(dx), 1 if near else 0, at)

            p0 = field(3, 0, 0, block)
            p_x = field(3, 1, 0, block - 1 + a)
            p_x1 = field(3, 1, 0, block + a)
            p_y1 = field(3, 0, 1, block)
            k1, k2, k3 = coupled(x, b, [main(0), main(1), main(2)])
            own_inv = inv[x, b]
            p_y = jnp.where(low, roll_rows(p_y1, 1), p_y1)
            g1 = own_inv * (force[0, x, b] + k1 + (p0 - p_x))
            g2 = own_inv * (force[1, x, b] + k2 + (p0 - p_y))
            g3 = own_inv * (force[2, x, b] + k3 + (p0 - below_z(p0)))
            (kx,) = coupled(x + 1, b, [xprime])
            inv_x = inv[x + 1, b]
            gx = inv_x * (force[0, x + 1, b] + kx + (p_x1 - p0))
            (ky,) = coupled(x, 1 - b, [yprime])
            inv_y = inv[x, 1 - b]
            gy = inv_y * (force[1, x, 1 - b] + ky + (p_y1 - jnp.where(low, p0, roll_rows(p0, 1))))
            spread = (gx - g1) + (jnp.where(low, gy, roll_rows(gy, -1)) - g2) + (above_z(g3) - g3)
            dp = jnp.where(zmask, spread * winv[x, b], 0.0)
            dp_y = jnp.where(low, dp, roll_rows(dp, 1))
            keep = 1.0 - DAMP
            u1 = field(0, 0, 0, block)
            u2 = field(1, 0, 0, block)
            u3 = field(2, 0, 0, block)
            ux = field(0, 1, 0, block + a)
            uy = field(1, 0, 1, block)
            push = own_inv * dp
            new_1 = jnp.where(zmask, keep * u1 + DAMP * (g1 + push), u1)
            new_2 = jnp.where(zmask, keep * u2 + DAMP * (g2 + push), u2)
            new_y = jnp.where(zmask & ymask, keep * uy + DAMP * (gy - inv_y * dp_y), uy)
            new_x = jnp.where(zmask, keep * ux + DAMP * (gx - inv_x * dp), ux)
            slots[base + 0, block + 1] = new_1
            slots[base + 1, block + 1] = new_2
            pack[0, block] = jnp.where(zmask, new_1, roll_lanes(new_x, 1))
            pack[1, block] = jnp.where(zmask, new_2, roll_lanes(new_y, 1))
            slots[base + 2, block + 1] = jnp.where(
                z3, keep * u3 + DAMP * (g3 + own_inv * (dp - below_z(dp))), u3
            )
            slots[base + 3, block + 1] = p0 + DAMP * dp
            slots[base + 4, block + 1] = new_y
            slots[base + 5, block + 1] = new_x
            return carry

        lax.fori_loop(0, 2, lambda n, t: block_step(1 + n * (blocks - 1), t), 0)

        def packed_tile(k, block):
            return pack.at[k, block] if k < 2 else slots.at[base + k, block + 1]

        for k in range(SENT):
            send_x[side, 0, k] = packed_tile(k, blocks)[...]
            send_x[side, 1, k] = packed_tile(k, 1)[...]
            for n in range(4):
                dx, dy = DIRECTIONS[4 + n]
                row = 6 if dy > 0 else 1
                source = packed_tile(k, blocks if dx > 0 else 1)
                send_c[side, n, k : k + 1] = source[row : row + 1]
        for n in (4, 5, 6, 7, 0, 1):
            guarded(present(n), lambda n=n: copy(n, side).start())
        lax.fori_loop(2, blocks, block_step, 0, unroll=2)
        for k in range(SENT):
            for block in range(1, blocks + 1):
                source = packed_tile(k, block)
                send_y[side, 0, k, block - 1 : block] = source[6:7]
                send_y[side, 1, k, block - 1 : block] = source[1:2]
        for n in (2, 3):
            guarded(present(n), lambda n=n: copy(n, side).start())
        for n in range(8):
            guarded(present(opposite(n)), lambda n=n: copy(n, side).wait_recv())

        for way, at, low_c, high_c in ((0, 1, 0, 1), (1, blocks + 2, 2, 3)):
            tiles = []
            for k in range(SENT):
                v = recv_x[side, way, k]
                v = jnp.where((rows == 0) & has_low, recv_c[side, low_c, k : k + 1], v)
                v = jnp.where((rows == 7) & has_high, recv_c[side, high_c, k : k + 1], v)
                tiles.append(v)
            x_index = jnp.minimum(at + a + shift[1, 0], blocks + 2)
            slots[base + 0, at] = jnp.where(zmask, tiles[0], field(0, 0, 0, at - 1))
            slots[base + 1, at] = jnp.where(zmask, tiles[1], field(1, 0, 0, at - 1))
            slots[base + 2, at] = tiles[2]
            slots[base + 3, at] = tiles[3]
            slots[base + 4, at] = jnp.where(
                zmask, roll_lanes(tiles[1], -1), field(1, 0, 1, at - 1)
            )
            slots[base + 5, at] = jnp.where(
                zmask, roll_lanes(tiles[0], -1), slots[rel[0, 1, 0], x_index]
            )

        zrow = zmask[0:1]

        def margin_rows(way, row):
            got = [recv_y[side, way, k] for k in range(SENT)]
            turned = [roll_lanes(got[0], -1), roll_lanes(got[1], -1)]
            for k, v, mixed in (
                (0, got[0], True),
                (1, got[1], True),
                (2, got[2], False),
                (3, got[3], False),
                (4, turned[1], True),
                (5, turned[0], True),
            ):
                for block in range(1, blocks + 1):
                    new_row = v[block - 1 : block]
                    if mixed:
                        new_row = jnp.where(zrow, new_row, slots[base + k, block + 1, row : row + 1])
                    slots[base + k, block + 1, row : row + 1] = new_row

        pl.when(has_low)(lambda: margin_rows(0, 0))
        pl.when(has_high)(lambda: margin_rows(1, 7))

        new = list(table)
        for xp in (0, 1):
            for yp in (0, 1):
                at = xp * 2 + yp
                same = (a == xp) & (b == yp)
                x_next = (a != xp) & (b == yp)
                y_next = (a == xp) & (b != yp)
                new[at] = jnp.where(same, base, jnp.where(x_next, base + 5, table[at]))
                new[16 + at] = jnp.where(same, 0, jnp.where(x_next, -a, table[16 + at]))
                new[4 + at] = jnp.where(same, base + 1, jnp.where(y_next, base + 4, table[4 + at]))
                new[8 + at] = jnp.where(same, base + 2, table[8 + at])
                new[12 + at] = jnp.where(same, base + 3, table[12 + at])
        return tuple(new)

    table = tuple(jnp.int32(n) for n in range(16)) + tuple(jnp.int32(0) for _ in range(4))
    table = lax.fori_loop(0, STEPS, sweep, table)

    def final(f, xp, yp, block):
        index = block + 1
        if f == 0:
            index = index + table[16 + xp * 2 + yp]
        return slots[table[f * 4 + xp * 2 + yp], index]

    def residual_sums(block, sums):
        sums = list(sums)
        for xp in (0, 1):
            for yp in (0, 1):
                x = 2 * block + xp

                def getter(f, xp=xp, yp=yp):
                    def get(dx, near):
                        at = block + (xp + dx) // 2
                        return final(f, (xp + dx) % 2, yp if near else 1 - yp, at)

                    return get

                ks = coupled(x, yp, [getter(0), getter(1), getter(2)])
                p0 = final(3, xp, yp, block)
                p_x = final(3, 1 - xp, yp, block - 1 + xp)
                p_y = final(3, xp, 1 - yp, block)
                if yp == 0:
                    p_y = roll_rows(p_y, 1)
                before = (p_x, p_y, below_z(p0))
                for d in range(3):
                    u = final(d, xp, yp, block)
                    mom = force[d, x, yp] - (diag[x, yp] * u - ks[d]) - (before[d] - p0)
                    sums[d] = sums[d] + mom
                sums[3] = sums[3] + vis[x, yp]
        return tuple(sums)

    odd_row = (rows & 1) == 1
    packed = []
    for half_no in range(2):
        zero = jnp.zeros(tile, jnp.float32)
        sums = lax.fori_loop(
            half_no * 4 + 1, half_no * 4 + 5, residual_sums, (zero, zero, zero, zero)
        )

        def collect(v):
            v = v + roll_rows(v, -1)
            v = v + roll_lanes(v, -1)
            return v + roll_lanes(v, -2)

        valid = odd_row & (rows < 7) & ((lanes & 3) == 0)
        below = jnp.where(valid, collect(sums[3]), 1.0)
        both = zero
        for d in range(3):
            value = jnp.where(valid, collect(sums[d]) / below, 0.0)
            both = both + (roll_lanes(value, d) if d else value)
        packed.append(both)
    own_part = packed[0] + roll_rows(packed[1], 1)
    shared[...] = own_part
    gathered[0] = own_part

    def spread_copy(hop):
        return pltpu.make_async_remote_copy(
            src_ref=shared,
            dst_ref=gathered.at[hop],
            send_sem=gsend_sem.at[hop],
            recv_sem=grecv_sem.at[hop],
            device_id=(lax.rem(lon + hop, lon_n), lat),
            device_id_type=MESH,
        )

    for hop in range(1, lon_n):
        spread_copy(hop).start()
    for hop in range(1, lon_n):
        spread_copy(hop).wait()

    for n in range(8):
        guarded(present(n), lambda n=n: first_copy(n).wait_send())

    def drain(s, carry):
        for n in range(8):
            guarded(present(n), lambda n=n: copy(n, s).wait_send())
        return carry

    lax.fori_loop(0, STEPS, drain, 0)

    cells = 2 * lon_n
    table_k = cycle_kernel(cells)
    smooth = []
    for half_no in range(2):
        total = jnp.zeros(tile, jnp.float32)
        for hop in range(lon_n):
            odd_k = table_k[(2 * hop + half_no) % cells]
            even_k = table_k[(2 * hop + half_no - 1) % cells]
            total = total + jnp.where(odd_row, odd_k, even_k) * gathered[hop]
        total = GAIN * (total + roll_rows(total, -1))
        per = []
        for d in range(3):
            v = jnp.where(odd_row & ((lanes & 3) == d), total, 0.0)
            if d:
                v = roll_lanes(v, -d)
            v = v + roll_lanes(v, 1)
            v = v + roll_lanes(v, 2)
            per.append(v + roll_rows(v, 1))
        smooth.append(per)

    for half_no in range(2):

        def finish(block, carry, half_no=half_no):
            for xp in (0, 1):
                for yp in (0, 1):
                    x = 2 * block + xp - 2
                    for d in range(3):
                        v = final(d, xp, yp, block) + smooth[half_no][d]
                        for row in range(6):
                            y = 2 * row + yp
                            vel_out[d, x, y : y + 1] = v[row + 1 : row + 2]
                    own = vis[x + 2, yp]
                    v = final(3, xp, yp, block) / jnp.where(own > 0, own, 1.0)
                    for row in range(6):
                        y = 2 * row + yp
                        p_out[x, y : y + 1] = v[row + 1 : row + 2]
            return carry

        lax.fori_loop(half_no * 4 + 1, half_no * 4 + 5, finish, 0)


def body(lon_n, lat_n, velocity, pressure_in, viscosity, body_force, colour_order):
    nx, ny, nz = viscosity.shape
    blocks = nx // 2
    f32 = jnp.float32
    whole = pl.BlockSpec(memory_space=pltpu.VMEM)
    n_slots = FIRST + NEW * STEPS
    return pl.pallas_call(
        functools.partial(kernel, lon_n, lat_n),
        out_shape=(
            jax.ShapeDtypeStruct((3, nx, ny, nz), f32),
            jax.ShapeDtypeStruct((nx, ny, nz), f32),
        ),
        in_specs=[pl.BlockSpec(memory_space=pltpu.SMEM)]
        + [pl.BlockSpec(memory_space=pl.ANY)] * 4,
        out_specs=(whole, whole),
        scratch_shapes=[
            pltpu.VMEM((3, nx, ny, nz), f32),
            pltpu.VMEM((nx, ny, nz), f32),
            pltpu.VMEM((nx, ny, nz), f32),
            pltpu.VMEM((3, nx, ny, nz), f32),
            pltpu.VMEM((nx + 4, 2, 8, nz), f32),
            pltpu.VMEM((3, nx + 4, 2, 8, nz), f32),
            pltpu.VMEM((n_slots, blocks + 3, 8, nz), f32),
            pltpu.VMEM((27, nx + 4, 2, 8, nz), f32),
            pltpu.VMEM((nx + 4, 2, 8, nz), f32),
            pltpu.VMEM((nx + 4, 2, 8, nz), f32),
            pltpu.VMEM((nx + 4, 2, 8, nz), f32),
            pltpu.VMEM((STEPS, 2, SENT, 8, nz), f32),
            pltpu.VMEM((STEPS, 2, SENT, 8, nz), f32),
            pltpu.VMEM((STEPS, 4, 8, nz), f32),
            pltpu.VMEM((STEPS, 2, SENT, 8, nz), f32),
            pltpu.VMEM((STEPS, 2, SENT, 8, nz), f32),
            pltpu.VMEM((STEPS, 4, 8, nz), f32),
            pltpu.VMEM((lon_n, 8, nz), f32),
            pltpu.VMEM((8, nz), f32),
            pltpu.VMEM((2, 16, 8, nz), f32),
            pltpu.VMEM((2, 13, nx, nz), f32),
            pltpu.VMEM((4, 16, nz), f32),
            pltpu.VMEM((2, 16, 8, nz), f32),
            pltpu.VMEM((2, 13, nx, nz), f32),
            pltpu.VMEM((4, 16, nz), f32),
            pltpu.SemaphoreType.DMA((8,)),
            pltpu.SemaphoreType.DMA((8,)),
            pltpu.VMEM((2, blocks + 1, 8, nz), f32),
            pltpu.SemaphoreType.DMA((4,)),
            pltpu.SemaphoreType.DMA((STEPS, 8)),
            pltpu.SemaphoreType.DMA((STEPS, 8)),
            pltpu.SemaphoreType.DMA((lon_n,)),
            pltpu.SemaphoreType.DMA((lon_n,)),
        ],
        compiler_params=pltpu.CompilerParams(
            collective_id=0, has_side_effects=True, vmem_limit_bytes=60 * 1024 * 1024
        ),
        name="vanka",
    )(colour_order, velocity, pressure_in, viscosity, body_force)


def solution(mesh):
    placed = (
        P(None, "lon", "lat", None),
        P("lon", "lat", None),
        P("lon", "lat", None),
        P(None, "lon", "lat", None),
        P(),
    )
    return jax.shard_map(
        functools.partial(body, mesh.shape["lon"], mesh.shape["lat"]),
        mesh=mesh,
        in_specs=placed,
        out_specs=(P(None, "lon", "lat", None), P("lon", "lat", None)),
        check_vma=False,
    )
```

```python
import functools
import math

import jax
import jax.numpy as jnp
from jax import lax
from jax.experimental import pallas as pl
from jax.experimental.pallas import tpu as pltpu
from jax.sharding import PartitionSpec as P

SWEEPS = 2
COLOURS = 8
STEPS = SWEEPS * COLOURS
DAMP = 0.6
GAIN = 0.25
SENT = 4
NEW = 6
FIRST = 16
MESH = pl.DeviceIdType.MESH
DIRECTIONS = ((1, 0), (-1, 0), (0, 1), (0, -1), (1, 1), (1, -1), (-1, 1), (-1, -1))


def opposite(n):
    return DIRECTIONS.index((-DIRECTIONS[n][0], -DIRECTIONS[n][1]))


def kslot(dx, dy, dz):
    return ((dx + 1) * 3 + (dy + 1)) * 3 + (dz + 1)


def cycle_kernel(cells):
    rate = 4.0 / cells
    screening = 2.0 * math.cosh(rate) - 2.0
    factor = screening / (2.0 * math.sinh(rate) * math.sinh(rate * cells / 2.0))
    return [factor * math.cosh(rate * (cells / 2.0 - d)) for d in range(cells)]


def kernel(
    lon_n,
    lat_n,
    order_ref,
    vel_hbm,
    p_hbm,
    vis_hbm,
    force_hbm,
    vel_out,
    p_out,
    vel_in,
    p_in,
    vis_in,
    force_in,
    vis,
    force,
    slots,
    coup,
    diag,
    inv,
    winv,
    send_x,
    send_y,
    send_c,
    recv_x,
    recv_y,
    recv_c,
    gathered,
    shared,
    first_send_x,
    first_send_y,
    first_send_c,
    first_recv_x,
    first_recv_y,
    first_recv_c,
    first_send_sem,
    first_recv_sem,
    pack,
    load_sem,
    send_sem,
    recv_sem,
    gsend_sem,
    grecv_sem,
):
    lon = lax.axis_index("lon")
    lat = lax.axis_index("lat")
    planes = vis.shape[0]
    depth = vis.shape[-1]
    blocks = planes // 2 - 2
    tile = (8, depth)
    rows = lax.broadcasted_iota(jnp.int32, tile, 0)
    lanes = lax.broadcasted_iota(jnp.int32, tile, 1)

    def roll_rows(v, up):
        return pltpu.roll(v, up % 8, 0)

    def roll_lanes(v, up):
        return pltpu.roll(v, up % depth, 1)

    def above_z(v):
        return jnp.where(lanes == depth - 1, 0.0, roll_lanes(v, -1))

    def below_z(v):
        return jnp.where(lanes == 0, 0.0, roll_lanes(v, 1))

    def partner(n):
        dx, dy = DIRECTIONS[n]
        return (lax.rem(lon + dx + lon_n, lon_n), lat + dy)

    def present(n):
        dy = DIRECTIONS[n][1]
        if dy > 0:
            return lat < lat_n - 1
        if dy < 0:
            return lat > 0
        return None

    def guarded(cond, fn):
        if cond is None:
            fn()
        else:
            pl.when(cond)(fn)

    pairs = ((vis_hbm, vis_in), (p_hbm, p_in), (vel_hbm, vel_in), (force_hbm, force_in))
    loads = [pltpu.make_async_copy(src, dst, load_sem.at[n]) for n, (src, dst) in enumerate(pairs)]
    for copy_in in loads:
        copy_in.start()

    barrier = pltpu.get_barrier_semaphore()
    for n in range(8):

        def greet(n=n):
            pl.semaphore_signal(barrier, inc=1, device_id=partner(n), device_id_type=MESH)

        guarded(present(n), greet)
    for hop in range(2, lon_n - 1):
        pl.semaphore_signal(
            barrier, inc=1, device_id=(lax.rem(lon + hop, lon_n), lat), device_id_type=MESH
        )

    blank = jnp.zeros(tile, jnp.float32)

    def clear(x, carry):
        for yp in (0, 1):
            vis[x, yp] = blank
            for d in range(3):
                force[d, x, yp] = blank
        return carry

    lax.fori_loop(0, planes, clear, 0)

    def clear_slots(at, carry):
        for n in range(FIRST):
            slots[n, at] = blank
        return carry

    lax.fori_loop(0, blocks + 3, clear_slots, 0)

    def split(block, carry):
        for xp in (0, 1):
            x = 2 * block + xp - 2
            seen = vis_in[x]
            scaled = p_in[x] * seen
            for y in range(12):
                yp, row = y % 2, y // 2 + 1
                vis[x + 2, yp, row : row + 1] = seen[y : y + 1]
                slots[12 + xp * 2 + yp, block + 1, row : row + 1] = scaled[y : y + 1]
                for d in range(3):
                    slots[d * 4 + xp * 2 + yp, block + 1, row : row + 1] = vel_in[d, x, y : y + 1]
                    force[d, x + 2, yp, row : row + 1] = force_in[d, x, y : y + 1]
        return carry

    for copy_in in loads:
        copy_in.wait()
    lax.fori_loop(1, blocks + 1, split, 0)

    def part(f, x, yp):
        if f == 7:
            return vis.at[x, yp]
        if f >= 4:
            return force.at[f - 4, x, yp]
        return slots.at[f * 4 + (x % 2) * 2 + yp, x // 2 + 1]

    first_x = (
        (
            [(7, 1, yp) for yp in (0, 1)],
            [(7, x, yp) for x in (planes - 2, planes - 1) for yp in (0, 1)],
        ),
        (
            [(f, 1, yp) for f in (0, 1, 2, 3) for yp in (0, 1)],
            [(f, planes - 2, yp) for f in (4, 0, 1, 2, 3) for yp in (0, 1)]
            + [(0, planes - 1, yp) for yp in (0, 1)],
        ),
    )
    first_y = (
        ([(7, 0), (7, 1)], [(7, 0), (7, 1)]),
        (
            [(f, 0) for f in (0, 1, 2, 3)] + [(f, 1) for f in (0, 1, 2, 3, 4, 5, 6)],
            [(f, 0) for f in (0, 1, 2, 3, 5)] + [(1, 1)],
        ),
    )
    own_planes = planes - 4

    def first_copy(part_no, n):
        if n < 2:
            at = (part_no, n, pl.ds(0, len(first_x[part_no][n])))
            src, dst = first_send_x.at[at], first_recv_x.at[at]
        elif n < 4:
            at = (part_no, n - 2, pl.ds(0, len(first_y[part_no][n - 2])))
            src, dst = first_send_y.at[at], first_recv_y.at[at]
        else:
            src, dst = first_send_c.at[part_no, n - 4], first_recv_c.at[part_no, n - 4]
        return pltpu.make_async_remote_copy(
            src_ref=src,
            dst_ref=dst,
            send_sem=first_send_sem.at[part_no, n],
            recv_sem=first_recv_sem.at[part_no, n],
            device_id=partner(n),
            device_id_type=MESH,
        )

    def first_stage(part_no):
        for way in (0, 1):
            for k, (f, x, yp) in enumerate(first_x[part_no][way]):
                source = part(f, x + own_planes if way == 0 else x - own_planes, yp)
                first_send_x[part_no, way, k] = source[...]
                for n in range(4):
                    dx, dy = DIRECTIONS[4 + n]
                    if (dx > 0) == (way == 0):
                        row = 6 if dy > 0 else 1
                        first_send_c[part_no, n, k : k + 1] = source[row : row + 1]
            row = 6 if way == 0 else 1
            for k, (f, yp) in enumerate(first_y[part_no][way]):
                for x in range(own_planes):
                    first_send_y[part_no, way, k, x : x + 1] = part(f, x + 2, yp)[
                        row : row + 1
                    ]

    def first_start(part_no):
        for n in (4, 5, 6, 7, 2, 3, 0, 1):
            guarded(present(n), lambda n=n: first_copy(part_no, n).start())

    has_low = lat > 0
    has_high = lat < lat_n - 1

    def first_finish(part_no):
        for n in range(8):
            guarded(present(opposite(n)), lambda n=n: first_copy(part_no, n).wait_recv())
        for way in (0, 1):
            low_c, high_c = (0, 1) if way == 0 else (2, 3)
            for k, (f, x, yp) in enumerate(first_x[part_no][way]):
                v = first_recv_x[part_no, way, k]
                v = jnp.where((rows == 0) & has_low, first_recv_c[part_no, low_c, k : k + 1], v)
                v = jnp.where((rows == 7) & has_high, first_recv_c[part_no, high_c, k : k + 1], v)
                part(f, x, yp)[...] = v

        def first_rows(way, row):
            for k, (f, yp) in enumerate(first_y[part_no][way]):
                for x in range(own_planes):
                    part(f, x + 2, yp)[row : row + 1] = first_recv_y[
                        part_no, way, k, x : x + 1
                    ]

        pl.when(has_low)(lambda: first_rows(0, 0))
        pl.when(has_high)(lambda: first_rows(1, 7))

    first_stage(0)
    ends = (lat == 0).astype(jnp.int32) + (lat == lat_n - 1).astype(jnp.int32)
    pl.semaphore_wait(barrier, lon_n + 5 - 3 * ends)
    first_start(0)
    first_stage(1)
    first_start(1)
    first_finish(0)

    def inside(yp):
        y = lat * 12 + 2 * (rows - 1) + yp
        return (y >= 0) & (y < 12 * lat_n)

    half = [(1, dy, dz) for dy in (-1, 0, 1) for dz in (-1, 0, 1)]
    half += [(0, 1, dz) for dz in (-1, 0, 1)] + [(0, 0, 1)]

    def couple(x, carry):
        for yp in (0, 1):
            own = vis[x, yp]
            for dx in (0, 1):
                for dy in (-1, 0, 1):
                    offsets = [o for o in half if o[0] == dx and o[1] == dy]
                    if not offsets:
                        continue
                    other_yp = yp if dy == 0 else 1 - yp
                    shift = 0
                    if dy == 1 and yp == 1:
                        shift = -1
                    if dy == -1 and yp == 0:
                        shift = 1
                    other = vis[x + dx, other_yp]
                    if shift:
                        other = roll_rows(other, shift)
                    for o in offsets:
                        dz = o[2]
                        beside = other
                        if dz == 1:
                            beside = above_z(other)
                        elif dz == -1:
                            beside = below_z(other)
                        reach = abs(dx) + abs(dy) + abs(dz)
                        scale = 2.0 * 0.5 ** (reach - 1)
                        value = (scale * own) * beside / jnp.maximum(own + beside, 1.0)
                        coup[kslot(*o), x, yp] = value
                        back = value
                        if dz:
                            back = roll_lanes(back, dz)
                        if shift:
                            back = roll_rows(back, -shift)
                        coup[kslot(-dx, -dy, -dz), x + dx, other_yp] = back
        return carry

    lax.fori_loop(1, planes - 1, couple, 0)

    def diagonal(x, carry):
        for yp in (0, 1):
            total = jnp.zeros(tile, jnp.float32)
            for n in range(27):
                if n != 13:
                    total = total + coup[n, x, yp]
            diag[x, yp] = total
            ok = inside(yp) & (total > 0)
            inv[x, yp] = jnp.where(ok, 1.0 / jnp.where(ok, total, 1.0), 0.0)
        return carry

    lax.fori_loop(2, planes - 1, diagonal, 0)

    def weights(x, carry):
        for yp in (0, 1):
            own = inv[x, yp]
            up = inv[x, 1 - yp]
            if yp == 1:
                up = roll_rows(up, -1)
            total = 3.0 * own + inv[x + 1, yp] + up + above_z(own)
            ok = inside(yp) & (total > 0)
            winv[x, yp] = jnp.where(ok, 1.0 / jnp.where(ok, total, 1.0), 0.0)
        return carry

    lax.fori_loop(2, planes - 2, weights, 0)
    first_finish(1)

    def coupled(x, t, fields):
        at_low = t == 0

        def turn(v):
            return jnp.where(at_low, roll_rows(v, 1), roll_rows(v, -1))

        sums = [[None] * 3 for _ in fields]

        def gather(dy, yp, near):
            for dx in (-1, 0, 1):
                tiles = [f(dx, near) for f in fields]
                for dz in (-1, 0, 1):
                    if near and dx == 0 and dz == 0:
                        continue
                    k = coup[((1 - dx) * 3 + (1 - dy)) * 3 + (1 - dz), x + dx, yp]
                    for n, v in enumerate(tiles):
                        term = k * v
                        old = sums[n][dz + 1]
                        sums[n][dz + 1] = term if old is None else old + term

        gather(jnp.where(at_low, -1, 1), 1 - t, 0)
        for n in range(len(fields)):
            sums[n] = [turn(v) for v in sums[n]]
        gather(jnp.where(at_low, 1, -1), 1 - t, 0)
        gather(0, t, 1)
        return [s[1] + roll_lanes(s[2], -1) + roll_lanes(s[0], 1) for s in sums]

    def pick(table, xp, yp):
        low = jnp.where(yp == 0, table[0], table[1])
        high = jnp.where(yp == 0, table[2], table[3])
        return jnp.where(xp == 0, low, high)

    def copy(n, side):
        if n < 2:
            src, dst = send_x.at[side, n], recv_x.at[side, n]
        elif n < 4:
            src, dst = send_y.at[side, n - 2], recv_y.at[side, n - 2]
        else:
            src, dst = send_c.at[side, n - 4], recv_c.at[side, n - 4]
        return pltpu.make_async_remote_copy(
            src_ref=src,
            dst_ref=dst,
            send_sem=send_sem.at[side, n],
            recv_sem=recv_sem.at[side, n],
            device_id=partner(n),
            device_id_type=MESH,
        )

    def sweep(s, table):
        colour = order_ref[lax.rem(s, COLOURS)]
        a = colour & 1
        b = (colour >> 1) & 1
        c = (colour >> 2) & 1
        base = FIRST + NEW * s
        side = s
        rel = {}
        for f in range(4):
            for xr in (0, 1):
                for yr in (0, 1):
                    rel[f, xr, yr] = pick(table[f * 4 : f * 4 + 4], a ^ xr, b ^ yr)
        shift = {
            (xr, yr): pick(table[16:20], a ^ xr, b ^ yr) for xr in (0, 1) for yr in (0, 1)
        }

        def field(f, xr, yr, block):
            index = block + 1
            if f == 0:
                index = index + shift[xr, yr]
            return slots[rel[f, xr, yr], index]

        zmask = (lanes & 1) == c
        z3 = (lanes > 0) | (c == 0)
        ymask = lat * 12 + 2 * (rows - 1) + (1 - b) >= 1
        low = b == 0

        def block_step(block, carry):
            x = 2 * block + a

            def main(f):
                def get(dx, near):
                    at = block if dx == 0 else (block - 1 + a if dx < 0 else block + a)
                    return field(f, abs(dx), 0 if near else 1, at)

                return get

            def xprime(dx, near):
                at = block + a if dx == 0 else (block if dx < 0 else block + 1)
                return field(0, 1 - abs(dx), 0 if near else 1, at)

            def yprime(dx, near):
                at = block if dx == 0 else (block - 1 + a if dx < 0 else block + a)
                return field(1, abs(dx), 1 if near else 0, at)

            p0 = field(3, 0, 0, block)
            p_x = field(3, 1, 0, block - 1 + a)
            p_x1 = field(3, 1, 0, block + a)
            p_y1 = field(3, 0, 1, block)
            k1, k2, k3 = coupled(x, b, [main(0), main(1), main(2)])
            own_inv = inv[x, b]
            p_y = jnp.where(low, roll_rows(p_y1, 1), p_y1)
            g1 = own_inv * (force[0, x, b] + k1 + (p0 - p_x))
            g2 = own_inv * (force[1, x, b] + k2 + (p0 - p_y))
            g3 = own_inv * (force[2, x, b] + k3 + (p0 - below_z(p0)))
            (kx,) = coupled(x + 1, b, [xprime])
            inv_x = inv[x + 1, b]
            gx = inv_x * (force[0, x + 1, b] + kx + (p_x1 - p0))
            (ky,) = coupled(x, 1 - b, [yprime])
            inv_y = inv[x, 1 - b]
            gy = inv_y * (force[1, x, 1 - b] + ky + (p_y1 - jnp.where(low, p0, roll_rows(p0, 1))))
            spread = (gx - g1) + (jnp.where(low, gy, roll_rows(gy, -1)) - g2) + (above_z(g3) - g3)
            dp = jnp.where(zmask, spread * winv[x, b], 0.0)
            dp_y = jnp.where(low, dp, roll_rows(dp, 1))
            keep = 1.0 - DAMP
            u1 = field(0, 0, 0, block)
            u2 = field(1, 0, 0, block)
            u3 = field(2, 0, 0, block)
            ux = field(0, 1, 0, block + a)
            uy = field(1, 0, 1, block)
            push = own_inv * dp
            new_1 = jnp.where(zmask, keep * u1 + DAMP * (g1 + push), u1)
            new_2 = jnp.where(zmask, keep * u2 + DAMP * (g2 + push), u2)
            new_y = jnp.where(zmask & ymask, keep * uy + DAMP * (gy - inv_y * dp_y), uy)
            new_x = jnp.where(zmask, keep * ux + DAMP * (gx - inv_x * dp), ux)
            slots[base + 0, block + 1] = new_1
            slots[base + 1, block + 1] = new_2
            pack[0, block] = jnp.where(zmask, new_1, roll_lanes(new_x, 1))
            pack[1, block] = jnp.where(zmask, new_2, roll_lanes(new_y, 1))
            slots[base + 2, block + 1] = jnp.where(
                z3, keep * u3 + DAMP * (g3 + own_inv * (dp - below_z(dp))), u3
            )
            slots[base + 3, block + 1] = p0 + DAMP * dp
            slots[base + 4, block + 1] = new_y
            slots[base + 5, block + 1] = new_x
            return carry

        lax.fori_loop(0, 2, lambda n, t: block_step(1 + n * (blocks - 1), t), 0)

        def packed_tile(k, block):
            return pack.at[k, block] if k < 2 else slots.at[base + k, block + 1]

        for k in range(SENT):
            send_x[side, 0, k] = packed_tile(k, blocks)[...]
            send_x[side, 1, k] = packed_tile(k, 1)[...]
            for n in range(4):
                dx, dy = DIRECTIONS[4 + n]
                row = 6 if dy > 0 else 1
                source = packed_tile(k, blocks if dx > 0 else 1)
                send_c[side, n, k : k + 1] = source[row : row + 1]
        for n in (4, 5, 6, 7, 0, 1):
            guarded(present(n), lambda n=n: copy(n, side).start())
        lax.fori_loop(2, blocks, block_step, 0, unroll=2)
        for k in range(SENT):
            for block in range(1, blocks + 1):
                source = packed_tile(k, block)
                send_y[side, 0, k, block - 1 : block] = source[6:7]
                send_y[side, 1, k, block - 1 : block] = source[1:2]
        for n in (2, 3):
            guarded(present(n), lambda n=n: copy(n, side).start())
        for n in range(8):
            guarded(present(opposite(n)), lambda n=n: copy(n, side).wait_recv())

        for way, at, low_c, high_c in ((0, 1, 0, 1), (1, blocks + 2, 2, 3)):
            tiles = []
            for k in range(SENT):
                v = recv_x[side, way, k]
                v = jnp.where((rows == 0) & has_low, recv_c[side, low_c, k : k + 1], v)
                v = jnp.where((rows == 7) & has_high, recv_c[side, high_c, k : k + 1], v)
                tiles.append(v)
            x_index = jnp.minimum(at + a + shift[1, 0], blocks + 2)
            slots[base + 0, at] = jnp.where(zmask, tiles[0], field(0, 0, 0, at - 1))
            slots[base + 1, at] = jnp.where(zmask, tiles[1], field(1, 0, 0, at - 1))
            slots[base + 2, at] = tiles[2]
            slots[base + 3, at] = tiles[3]
            slots[base + 4, at] = jnp.where(
                zmask, roll_lanes(tiles[1], -1), field(1, 0, 1, at - 1)
            )
            slots[base + 5, at] = jnp.where(
                zmask, roll_lanes(tiles[0], -1), slots[rel[0, 1, 0], x_index]
            )

        zrow = zmask[0:1]

        def margin_rows(way, row):
            got = [recv_y[side, way, k] for k in range(SENT)]
            turned = [roll_lanes(got[0], -1), roll_lanes(got[1], -1)]
            for k, v, mixed in (
                (0, got[0], True),
                (1, got[1], True),
                (2, got[2], False),
                (3, got[3], False),
                (4, turned[1], True),
                (5, turned[0], True),
            ):
                for block in range(1, blocks + 1):
                    new_row = v[block - 1 : block]
                    if mixed:
                        new_row = jnp.where(zrow, new_row, slots[base + k, block + 1, row : row + 1])
                    slots[base + k, block + 1, row : row + 1] = new_row

        pl.when(has_low)(lambda: margin_rows(0, 0))
        pl.when(has_high)(lambda: margin_rows(1, 7))

        new = list(table)
        for xp in (0, 1):
            for yp in (0, 1):
                at = xp * 2 + yp
                same = (a == xp) & (b == yp)
                x_next = (a != xp) & (b == yp)
                y_next = (a == xp) & (b != yp)
                new[at] = jnp.where(same, base, jnp.where(x_next, base + 5, table[at]))
                new[16 + at] = jnp.where(same, 0, jnp.where(x_next, -a, table[16 + at]))
                new[4 + at] = jnp.where(same, base + 1, jnp.where(y_next, base + 4, table[4 + at]))
                new[8 + at] = jnp.where(same, base + 2, table[8 + at])
                new[12 + at] = jnp.where(same, base + 3, table[12 + at])
        return tuple(new)

    table = tuple(jnp.int32(n) for n in range(16)) + tuple(jnp.int32(0) for _ in range(4))
    table = lax.fori_loop(0, STEPS, sweep, table)

    def final(f, xp, yp, block):
        index = block + 1
        if f == 0:
            index = index + table[16 + xp * 2 + yp]
        return slots[table[f * 4 + xp * 2 + yp], index]

    def residual_sums(block, sums):
        sums = list(sums)
        for xp in (0, 1):
            for yp in (0, 1):
                x = 2 * block + xp

                def getter(f, xp=xp, yp=yp):
                    def get(dx, near):
                        at = block + (xp + dx) // 2
                        return final(f, (xp + dx) % 2, yp if near else 1 - yp, at)

                    return get

                ks = coupled(x, yp, [getter(0), getter(1), getter(2)])
                p0 = final(3, xp, yp, block)
                p_x = final(3, 1 - xp, yp, block - 1 + xp)
                p_y = final(3, xp, 1 - yp, block)
                if yp == 0:
                    p_y = roll_rows(p_y, 1)
                before = (p_x, p_y, below_z(p0))
                for d in range(3):
                    u = final(d, xp, yp, block)
                    mom = force[d, x, yp] - (diag[x, yp] * u - ks[d]) - (before[d] - p0)
                    sums[d] = sums[d] + mom
                sums[3] = sums[3] + vis[x, yp]
        return tuple(sums)

    odd_row = (rows & 1) == 1
    packed = []
    for half_no in range(2):
        zero = jnp.zeros(tile, jnp.float32)
        sums = lax.fori_loop(
            half_no * 4 + 1, half_no * 4 + 5, residual_sums, (zero, zero, zero, zero)
        )

        def collect(v):
            v = v + roll_rows(v, -1)
            v = v + roll_lanes(v, -1)
            return v + roll_lanes(v, -2)

        valid = odd_row & (rows < 7) & ((lanes & 3) == 0)
        below = jnp.where(valid, collect(sums[3]), 1.0)
        both = zero
        for d in range(3):
            value = jnp.where(valid, collect(sums[d]) / below, 0.0)
            both = both + (roll_lanes(value, d) if d else value)
        packed.append(both)
    own_part = packed[0] + roll_rows(packed[1], 1)
    shared[...] = own_part
    gathered[0] = own_part

    def spread_copy(hop):
        return pltpu.make_async_remote_copy(
            src_ref=shared,
            dst_ref=gathered.at[hop],
            send_sem=gsend_sem.at[hop],
            recv_sem=grecv_sem.at[hop],
            device_id=(lax.rem(lon + hop, lon_n), lat),
            device_id_type=MESH,
        )

    for hop in range(1, lon_n):
        spread_copy(hop).start()
    for hop in range(1, lon_n):
        spread_copy(hop).wait()

    for part_no in (0, 1):
        for n in range(8):
            guarded(present(n), lambda p=part_no, n=n: first_copy(p, n).wait_send())

    def drain(s, carry):
        for n in range(8):
            guarded(present(n), lambda n=n: copy(n, s).wait_send())
        return carry

    lax.fori_loop(0, STEPS, drain, 0)

    cells = 2 * lon_n
    table_k = cycle_kernel(cells)
    smooth = []
    for half_no in range(2):
        total = jnp.zeros(tile, jnp.float32)
        for hop in range(lon_n):
            odd_k = table_k[(2 * hop + half_no) % cells]
            even_k = table_k[(2 * hop + half_no - 1) % cells]
            total = total + jnp.where(odd_row, odd_k, even_k) * gathered[hop]
        total = GAIN * (total + roll_rows(total, -1))
        per = []
        for d in range(3):
            v = jnp.where(odd_row & ((lanes & 3) == d), total, 0.0)
            if d:
                v = roll_lanes(v, -d)
            v = v + roll_lanes(v, 1)
            v = v + roll_lanes(v, 2)
            per.append(v + roll_rows(v, 1))
        smooth.append(per)

    for half_no in range(2):

        def finish(block, carry, half_no=half_no):
            for xp in (0, 1):
                for yp in (0, 1):
                    x = 2 * block + xp - 2
                    for d in range(3):
                        v = final(d, xp, yp, block) + smooth[half_no][d]
                        for row in range(6):
                            y = 2 * row + yp
                            vel_out[d, x, y : y + 1] = v[row + 1 : row + 2]
                    own = vis[x + 2, yp]
                    v = final(3, xp, yp, block) / jnp.where(own > 0, own, 1.0)
                    for row in range(6):
                        y = 2 * row + yp
                        p_out[x, y : y + 1] = v[row + 1 : row + 2]
            return carry

        lax.fori_loop(half_no * 4 + 1, half_no * 4 + 5, finish, 0)


def body(lon_n, lat_n, velocity, pressure_in, viscosity, body_force, colour_order):
    nx, ny, nz = viscosity.shape
    blocks = nx // 2
    f32 = jnp.float32
    whole = pl.BlockSpec(memory_space=pltpu.VMEM)
    n_slots = FIRST + NEW * STEPS
    return pl.pallas_call(
        functools.partial(kernel, lon_n, lat_n),
        out_shape=(
            jax.ShapeDtypeStruct((3, nx, ny, nz), f32),
            jax.ShapeDtypeStruct((nx, ny, nz), f32),
        ),
        in_specs=[pl.BlockSpec(memory_space=pltpu.SMEM)]
        + [pl.BlockSpec(memory_space=pl.ANY)] * 4,
        out_specs=(whole, whole),
        scratch_shapes=[
            pltpu.VMEM((3, nx, ny, nz), f32),
            pltpu.VMEM((nx, ny, nz), f32),
            pltpu.VMEM((nx, ny, nz), f32),
            pltpu.VMEM((3, nx, ny, nz), f32),
            pltpu.VMEM((nx + 4, 2, 8, nz), f32),
            pltpu.VMEM((3, nx + 4, 2, 8, nz), f32),
            pltpu.VMEM((n_slots, blocks + 3, 8, nz), f32),
            pltpu.VMEM((27, nx + 4, 2, 8, nz), f32),
            pltpu.VMEM((nx + 4, 2, 8, nz), f32),
            pltpu.VMEM((nx + 4, 2, 8, nz), f32),
            pltpu.VMEM((nx + 4, 2, 8, nz), f32),
            pltpu.VMEM((STEPS, 2, SENT, 8, nz), f32),
            pltpu.VMEM((STEPS, 2, SENT, 8, nz), f32),
            pltpu.VMEM((STEPS, 4, 8, nz), f32),
            pltpu.VMEM((STEPS, 2, SENT, 8, nz), f32),
            pltpu.VMEM((STEPS, 2, SENT, 8, nz), f32),
            pltpu.VMEM((STEPS, 4, 8, nz), f32),
            pltpu.VMEM((lon_n, 8, nz), f32),
            pltpu.VMEM((8, nz), f32),
            pltpu.VMEM((2, 2, 12, 8, nz), f32),
            pltpu.VMEM((2, 2, 11, nx, nz), f32),
            pltpu.VMEM((2, 4, 16, nz), f32),
            pltpu.VMEM((2, 2, 12, 8, nz), f32),
            pltpu.VMEM((2, 2, 11, nx, nz), f32),
            pltpu.VMEM((2, 4, 16, nz), f32),
            pltpu.SemaphoreType.DMA((2, 8)),
            pltpu.SemaphoreType.DMA((2, 8)),
            pltpu.VMEM((2, blocks + 1, 8, nz), f32),
            pltpu.SemaphoreType.DMA((4,)),
            pltpu.SemaphoreType.DMA((STEPS, 8)),
            pltpu.SemaphoreType.DMA((STEPS, 8)),
            pltpu.SemaphoreType.DMA((lon_n,)),
            pltpu.SemaphoreType.DMA((lon_n,)),
        ],
        compiler_params=pltpu.CompilerParams(
            collective_id=0, has_side_effects=True, vmem_limit_bytes=60 * 1024 * 1024
        ),
        name="vanka",
    )(colour_order, velocity, pressure_in, viscosity, body_force)


def solution(mesh):
    placed = (
        P(None, "lon", "lat", None),
        P("lon", "lat", None),
        P("lon", "lat", None),
        P(None, "lon", "lat", None),
        P(),
    )
    return jax.shard_map(
        functools.partial(body, mesh.shape["lon"], mesh.shape["lat"]),
        mesh=mesh,
        in_specs=placed,
        out_specs=(P(None, "lon", "lat", None), P("lon", "lat", None)),
        check_vma=False,
    )
```

```python
import functools
import math

import jax
import jax.numpy as jnp
from jax import lax
from jax.experimental import pallas as pl
from jax.experimental.pallas import tpu as pltpu
from jax.sharding import PartitionSpec as P

SWEEPS = 2
COLOURS = 8
STEPS = SWEEPS * COLOURS
DAMP = 0.6
GAIN = 0.25
NEAR_ROWS, MID_ROWS = 24, 16
SENT = 4
NEW = 6
FIRST = 16
MESH = pl.DeviceIdType.MESH
DIRECTIONS = ((1, 0), (-1, 0), (0, 1), (0, -1), (1, 1), (1, -1), (-1, 1), (-1, -1), (0, 1), (0, -1))


def opposite(n):
    return DIRECTIONS.index((-DIRECTIONS[n][0], -DIRECTIONS[n][1]))


def kslot(dx, dy, dz):
    return ((dx + 1) * 3 + (dy + 1)) * 3 + (dz + 1)


def cycle_kernel(cells):
    rate = 4.0 / cells
    screening = 2.0 * math.cosh(rate) - 2.0
    factor = screening / (2.0 * math.sinh(rate) * math.sinh(rate * cells / 2.0))
    return [factor * math.cosh(rate * (cells / 2.0 - d)) for d in range(cells)]


def kernel(
    lon_n,
    lat_n,
    order_ref,
    vel_hbm,
    p_hbm,
    vis_hbm,
    force_hbm,
    vel_out,
    p_out,
    vel_in,
    p_in,
    vis_in,
    force_in,
    vis,
    force,
    slots,
    coup,
    diag,
    inv,
    winv,
    send_x,
    send_y,
    send_c,
    recv_x,
    recv_y,
    recv_c,
    gathered,
    shared,
    first_send_x,
    first_send_y,
    first_send_c,
    first_recv_x,
    first_recv_y,
    first_recv_c,
    first_send_sem,
    first_recv_sem,
    send_mid,
    recv_mid,
    pack,
    load_sem,
    send_sem,
    recv_sem,
    gsend_sem,
    grecv_sem,
):
    lon = lax.axis_index("lon")
    lat = lax.axis_index("lat")
    planes = vis.shape[0]
    depth = vis.shape[-1]
    blocks = planes // 2 - 2
    tile = (8, depth)
    rows = lax.broadcasted_iota(jnp.int32, tile, 0)
    lanes = lax.broadcasted_iota(jnp.int32, tile, 1)

    def roll_rows(v, up):
        return pltpu.roll(v, up % 8, 0)

    def roll_lanes(v, up):
        return pltpu.roll(v, up % depth, 1)

    def above_z(v):
        return jnp.where(lanes == depth - 1, 0.0, roll_lanes(v, -1))

    def below_z(v):
        return jnp.where(lanes == 0, 0.0, roll_lanes(v, 1))

    def partner(n):
        dx, dy = DIRECTIONS[n]
        return (lax.rem(lon + dx + lon_n, lon_n), lat + dy)

    def present(n):
        dy = DIRECTIONS[n][1]
        if dy > 0:
            return lat < lat_n - 1
        if dy < 0:
            return lat > 0
        return None

    def guarded(cond, fn):
        if cond is None:
            fn()
        else:
            pl.when(cond)(fn)

    pairs = ((vis_hbm, vis_in), (p_hbm, p_in), (vel_hbm, vel_in), (force_hbm, force_in))
    loads = [pltpu.make_async_copy(src, dst, load_sem.at[n]) for n, (src, dst) in enumerate(pairs)]
    for copy_in in loads:
        copy_in.start()

    barrier = pltpu.get_barrier_semaphore()
    for n in range(8):

        def greet(n=n):
            pl.semaphore_signal(barrier, inc=1, device_id=partner(n), device_id_type=MESH)

        guarded(present(n), greet)
    for hop in range(2, lon_n - 1):
        pl.semaphore_signal(
            barrier, inc=1, device_id=(lax.rem(lon + hop, lon_n), lat), device_id_type=MESH
        )

    blank = jnp.zeros(tile, jnp.float32)

    def clear(x, carry):
        for yp in (0, 1):
            vis[x, yp] = blank
            for d in range(3):
                force[d, x, yp] = blank
        return carry

    lax.fori_loop(0, planes, clear, 0)

    def clear_slots(at, carry):
        for n in range(FIRST):
            slots[n, at] = blank
        return carry

    lax.fori_loop(0, blocks + 3, clear_slots, 0)

    def split(block, carry):
        for xp in (0, 1):
            x = 2 * block + xp - 2
            seen = vis_in[x]
            scaled = p_in[x] * seen
            for y in range(12):
                yp, row = y % 2, y // 2 + 1
                vis[x + 2, yp, row : row + 1] = seen[y : y + 1]
                slots[12 + xp * 2 + yp, block + 1, row : row + 1] = scaled[y : y + 1]
                for d in range(3):
                    slots[d * 4 + xp * 2 + yp, block + 1, row : row + 1] = vel_in[d, x, y : y + 1]
                    force[d, x + 2, yp, row : row + 1] = force_in[d, x, y : y + 1]
        return carry

    for copy_in in loads:
        copy_in.wait()
    lax.fori_loop(1, blocks + 1, split, 0)

    def part(f, x, yp):
        if f == 7:
            return vis.at[x, yp]
        if f >= 4:
            return force.at[f - 4, x, yp]
        return slots.at[f * 4 + (x % 2) * 2 + yp, x // 2 + 1]

    first_x = (
        (
            [(7, 1, yp) for yp in (0, 1)],
            [(7, x, yp) for x in (planes - 2, planes - 1) for yp in (0, 1)],
        ),
        (
            [(f, 1, yp) for f in (0, 1, 2, 3) for yp in (0, 1)],
            [(f, planes - 2, yp) for f in (4, 0, 1, 2, 3) for yp in (0, 1)]
            + [(0, planes - 1, yp) for yp in (0, 1)],
        ),
    )
    first_y = (
        ([(7, 0), (7, 1)], [(7, 0), (7, 1)]),
        (
            [(f, 0) for f in (0, 1, 2, 3)] + [(f, 1) for f in (0, 1, 2, 3, 4, 5, 6)],
            [(f, 0) for f in (0, 1, 2, 3, 5)] + [(1, 1)],
        ),
    )
    own_planes = planes - 4

    def first_copy(part_no, n):
        if n < 2:
            at = (part_no, n, pl.ds(0, len(first_x[part_no][n])))
            src, dst = first_send_x.at[at], first_recv_x.at[at]
        elif n < 4:
            at = (part_no, n - 2, pl.ds(0, len(first_y[part_no][n - 2])))
            src, dst = first_send_y.at[at], first_recv_y.at[at]
        else:
            src, dst = first_send_c.at[part_no, n - 4], first_recv_c.at[part_no, n - 4]
        return pltpu.make_async_remote_copy(
            src_ref=src,
            dst_ref=dst,
            send_sem=first_send_sem.at[part_no, n],
            recv_sem=first_recv_sem.at[part_no, n],
            device_id=partner(n),
            device_id_type=MESH,
        )

    def first_stage(part_no):
        for way in (0, 1):
            for k, (f, x, yp) in enumerate(first_x[part_no][way]):
                source = part(f, x + own_planes if way == 0 else x - own_planes, yp)
                first_send_x[part_no, way, k] = source[...]
                for n in range(4):
                    dx, dy = DIRECTIONS[4 + n]
                    if (dx > 0) == (way == 0):
                        row = 6 if dy > 0 else 1
                        first_send_c[part_no, n, k : k + 1] = source[row : row + 1]
            row = 6 if way == 0 else 1
            for k, (f, yp) in enumerate(first_y[part_no][way]):
                for x in range(own_planes):
                    first_send_y[part_no, way, k, x : x + 1] = part(f, x + 2, yp)[
                        row : row + 1
                    ]

    def first_start(part_no):
        for n in (4, 5, 6, 7, 2, 3, 0, 1):
            guarded(present(n), lambda n=n: first_copy(part_no, n).start())

    has_low = lat > 0
    has_high = lat < lat_n - 1

    def first_finish(part_no):
        for n in range(8):
            guarded(present(opposite(n)), lambda n=n: first_copy(part_no, n).wait_recv())
        for way in (0, 1):
            low_c, high_c = (0, 1) if way == 0 else (2, 3)
            for k, (f, x, yp) in enumerate(first_x[part_no][way]):
                v = first_recv_x[part_no, way, k]
                v = jnp.where((rows == 0) & has_low, first_recv_c[part_no, low_c, k : k + 1], v)
                v = jnp.where((rows == 7) & has_high, first_recv_c[part_no, high_c, k : k + 1], v)
                part(f, x, yp)[...] = v

        def first_rows(way, row):
            for k, (f, yp) in enumerate(first_y[part_no][way]):
                for x in range(own_planes):
                    part(f, x + 2, yp)[row : row + 1] = first_recv_y[
                        part_no, way, k, x : x + 1
                    ]

        pl.when(has_low)(lambda: first_rows(0, 0))
        pl.when(has_high)(lambda: first_rows(1, 7))

    first_stage(0)
    ends = (lat == 0).astype(jnp.int32) + (lat == lat_n - 1).astype(jnp.int32)
    pl.semaphore_wait(barrier, lon_n + 5 - 3 * ends)
    first_start(0)
    first_stage(1)
    first_start(1)
    first_finish(0)

    def inside(yp):
        y = lat * 12 + 2 * (rows - 1) + yp
        return (y >= 0) & (y < 12 * lat_n)

    half = [(1, dy, dz) for dy in (-1, 0, 1) for dz in (-1, 0, 1)]
    half += [(0, 1, dz) for dz in (-1, 0, 1)] + [(0, 0, 1)]

    def couple(x, carry):
        for yp in (0, 1):
            own = vis[x, yp]
            for dx in (0, 1):
                for dy in (-1, 0, 1):
                    offsets = [o for o in half if o[0] == dx and o[1] == dy]
                    if not offsets:
                        continue
                    other_yp = yp if dy == 0 else 1 - yp
                    shift = 0
                    if dy == 1 and yp == 1:
                        shift = -1
                    if dy == -1 and yp == 0:
                        shift = 1
                    other = vis[x + dx, other_yp]
                    if shift:
                        other = roll_rows(other, shift)
                    for o in offsets:
                        dz = o[2]
                        beside = other
                        if dz == 1:
                            beside = above_z(other)
                        elif dz == -1:
                            beside = below_z(other)
                        reach = abs(dx) + abs(dy) + abs(dz)
                        scale = 2.0 * 0.5 ** (reach - 1)
                        value = (scale * own) * beside / jnp.maximum(own + beside, 1.0)
                        coup[kslot(*o), x, yp] = value
                        back = value
                        if dz:
                            back = roll_lanes(back, dz)
                        if shift:
                            back = roll_rows(back, -shift)
                        coup[kslot(-dx, -dy, -dz), x + dx, other_yp] = back
        return carry

    lax.fori_loop(1, planes - 1, couple, 0)

    def diagonal(x, carry):
        for yp in (0, 1):
            total = jnp.zeros(tile, jnp.float32)
            for n in range(27):
                if n != 13:
                    total = total + coup[n, x, yp]
            diag[x, yp] = total
            ok = inside(yp) & (total > 0)
            inv[x, yp] = jnp.where(ok, 1.0 / jnp.where(ok, total, 1.0), 0.0)
        return carry

    lax.fori_loop(2, planes - 1, diagonal, 0)

    def weights(x, carry):
        for yp in (0, 1):
            own = inv[x, yp]
            up = inv[x, 1 - yp]
            if yp == 1:
                up = roll_rows(up, -1)
            total = 3.0 * own + inv[x + 1, yp] + up + above_z(own)
            ok = inside(yp) & (total > 0)
            winv[x, yp] = jnp.where(ok, 1.0 / jnp.where(ok, total, 1.0), 0.0)
        return carry

    lax.fori_loop(2, planes - 2, weights, 0)
    first_finish(1)

    def coupled(x, t, fields):
        at_low = t == 0

        def turn(v):
            return jnp.where(at_low, roll_rows(v, 1), roll_rows(v, -1))

        sums = [[None] * 3 for _ in fields]

        def gather(dy, yp, near):
            for dx in (-1, 0, 1):
                tiles = [f(dx, near) for f in fields]
                for dz in (-1, 0, 1):
                    if near and dx == 0 and dz == 0:
                        continue
                    k = coup[((1 - dx) * 3 + (1 - dy)) * 3 + (1 - dz), x + dx, yp]
                    for n, v in enumerate(tiles):
                        term = k * v
                        old = sums[n][dz + 1]
                        sums[n][dz + 1] = term if old is None else old + term

        gather(jnp.where(at_low, -1, 1), 1 - t, 0)
        for n in range(len(fields)):
            sums[n] = [turn(v) for v in sums[n]]
        gather(jnp.where(at_low, 1, -1), 1 - t, 0)
        gather(0, t, 1)
        return [s[1] + roll_lanes(s[2], -1) + roll_lanes(s[0], 1) for s in sums]

    def pick(table, xp, yp):
        low = jnp.where(yp == 0, table[0], table[1])
        high = jnp.where(yp == 0, table[2], table[3])
        return jnp.where(xp == 0, low, high)

    def copy(n, side):
        if n < 2:
            src, dst = send_x.at[side, n], recv_x.at[side, n]
        elif n < 4:
            src, dst = send_y.at[side, n - 2], recv_y.at[side, n - 2]
        elif n >= 8:
            src, dst = send_mid.at[side, n - 8], recv_mid.at[side, n - 8]
        else:
            src, dst = send_c.at[side, n - 4], recv_c.at[side, n - 4]
        return pltpu.make_async_remote_copy(
            src_ref=src,
            dst_ref=dst,
            send_sem=send_sem.at[side, n],
            recv_sem=recv_sem.at[side, n],
            device_id=partner(n),
            device_id_type=MESH,
        )

    near = (1, 2, blocks - 2, blocks - 1, blocks)
    mid = tuple(range(3, blocks - 2))

    def margin_rows(side, which, way, row):
        base = FIRST + NEW * side
        z_parity = (order_ref[lax.rem(side, COLOURS)] >> 2) & 1
        zrow = (lanes[0:1] & 1) == z_parity
        buffer, group = (recv_y, near) if which == 0 else (recv_mid, mid)
        per = len(group)
        got = buffer[side, way]
        turned = roll_lanes(got[0:16], -1)
        for k, v, at, mixed in (
            (0, got, 0, True),
            (1, got, per, True),
            (2, got, 2 * per, False),
            (3, got, 3 * per, False),
            (4, turned, per, True),
            (5, turned, 0, True),
        ):
            for n, block in enumerate(group):
                new_row = v[at + n : at + n + 1]
                if mixed:
                    new_row = jnp.where(zrow, new_row, slots[base + k, block + 1, row : row + 1])
                slots[base + k, block + 1, row : row + 1] = new_row

    def finish_mid(side):
        for n in (8, 9):
            guarded(present(opposite(n)), lambda n=n: copy(n, side).wait_recv())
        pl.when(has_low)(lambda: margin_rows(side, 1, 0, 0))
        pl.when(has_high)(lambda: margin_rows(side, 1, 1, 7))

    def prepare(s, table):
        colour = order_ref[lax.rem(s, COLOURS)]
        a = colour & 1
        b = (colour >> 1) & 1
        c = (colour >> 2) & 1
        base = FIRST + NEW * s
        side = s
        rel = {}
        for f in range(4):
            for xr in (0, 1):
                for yr in (0, 1):
                    rel[f, xr, yr] = pick(table[f * 4 : f * 4 + 4], a ^ xr, b ^ yr)
        shift = {
            (xr, yr): pick(table[16:20], a ^ xr, b ^ yr) for xr in (0, 1) for yr in (0, 1)
        }

        def field(f, xr, yr, block):
            index = block + 1
            if f == 0:
                index = index + shift[xr, yr]
            return slots[rel[f, xr, yr], index]

        zmask = (lanes & 1) == c
        z3 = (lanes > 0) | (c == 0)
        ymask = lat * 12 + 2 * (rows - 1) + (1 - b) >= 1
        low = b == 0

        def block_step(block, carry):
            x = 2 * block + a

            def main(f):
                def get(dx, near):
                    at = block if dx == 0 else (block - 1 + a if dx < 0 else block + a)
                    return field(f, abs(dx), 0 if near else 1, at)

                return get

            def xprime(dx, near):
                at = block + a if dx == 0 else (block if dx < 0 else block + 1)
                return field(0, 1 - abs(dx), 0 if near else 1, at)

            def yprime(dx, near):
                at = block if dx == 0 else (block - 1 + a if dx < 0 else block + a)
                return field(1, abs(dx), 1 if near else 0, at)

            p0 = field(3, 0, 0, block)
            p_x = field(3, 1, 0, block - 1 + a)
            p_x1 = field(3, 1, 0, block + a)
            p_y1 = field(3, 0, 1, block)
            k1, k2, k3 = coupled(x, b, [main(0), main(1), main(2)])
            own_inv = inv[x, b]
            p_y = jnp.where(low, roll_rows(p_y1, 1), p_y1)
            g1 = own_inv * (force[0, x, b] + k1 + (p0 - p_x))
            g2 = own_inv * (force[1, x, b] + k2 + (p0 - p_y))
            g3 = own_inv * (force[2, x, b] + k3 + (p0 - below_z(p0)))
            (kx,) = coupled(x + 1, b, [xprime])
            inv_x = inv[x + 1, b]
            gx = inv_x * (force[0, x + 1, b] + kx + (p_x1 - p0))
            (ky,) = coupled(x, 1 - b, [yprime])
            inv_y = inv[x, 1 - b]
            gy = inv_y * (force[1, x, 1 - b] + ky + (p_y1 - jnp.where(low, p0, roll_rows(p0, 1))))
            spread = (gx - g1) + (jnp.where(low, gy, roll_rows(gy, -1)) - g2) + (above_z(g3) - g3)
            dp = jnp.where(zmask, spread * winv[x, b], 0.0)
            dp_y = jnp.where(low, dp, roll_rows(dp, 1))
            keep = 1.0 - DAMP
            u1 = field(0, 0, 0, block)
            u2 = field(1, 0, 0, block)
            u3 = field(2, 0, 0, block)
            ux = field(0, 1, 0, block + a)
            uy = field(1, 0, 1, block)
            push = own_inv * dp
            new_1 = jnp.where(zmask, keep * u1 + DAMP * (g1 + push), u1)
            new_2 = jnp.where(zmask, keep * u2 + DAMP * (g2 + push), u2)
            new_y = jnp.where(zmask & ymask, keep * uy + DAMP * (gy - inv_y * dp_y), uy)
            new_x = jnp.where(zmask, keep * ux + DAMP * (gx - inv_x * dp), ux)
            slots[base + 0, block + 1] = new_1
            slots[base + 1, block + 1] = new_2
            pack[0, block] = jnp.where(zmask, new_1, roll_lanes(new_x, 1))
            pack[1, block] = jnp.where(zmask, new_2, roll_lanes(new_y, 1))
            slots[base + 2, block + 1] = jnp.where(
                z3, keep * u3 + DAMP * (g3 + own_inv * (dp - below_z(dp))), u3
            )
            slots[base + 3, block + 1] = p0 + DAMP * dp
            slots[base + 4, block + 1] = new_y
            slots[base + 5, block + 1] = new_x
            return carry

        def packed_tile(k, block):
            return pack.at[k, block] if k < 2 else slots.at[base + k, block + 1]

        def edge():
            lax.fori_loop(0, 2, lambda n, t: block_step(1 + n * (blocks - 1), t), 0)

            for k in range(SENT):
                send_x[side, 0, k] = packed_tile(k, blocks)[...]
                send_x[side, 1, k] = packed_tile(k, 1)[...]
                for n in range(4):
                    dx, dy = DIRECTIONS[4 + n]
                    row = 6 if dy > 0 else 1
                    source = packed_tile(k, blocks if dx > 0 else 1)
                    send_c[side, n, k : k + 1] = source[row : row + 1]
            for n in (4, 5, 6, 7, 0, 1):
                guarded(present(n), lambda n=n: copy(n, side).start())

        def inner():
            for block in (2, blocks - 2, blocks - 1):
                block_step(block, 0)

            def stage_rows(buffer, group):
                for k in range(SENT):
                    for n, block in enumerate(group):
                        at = k * len(group) + n
                        source = packed_tile(k, block)
                        buffer[side, 0, at : at + 1] = source[6:7]
                        buffer[side, 1, at : at + 1] = source[1:2]

            stage_rows(send_y, near)
            for n in (2, 3):
                guarded(present(n), lambda n=n: copy(n, side).start())
            lax.fori_loop(3, blocks - 2, block_step, 0)
            stage_rows(send_mid, mid)
            for n in (8, 9):
                guarded(present(n), lambda n=n: copy(n, side).start())

        def receive():
            for n in range(8):
                guarded(present(opposite(n)), lambda n=n: copy(n, side).wait_recv())

            for way, at, low_c, high_c in ((0, 1, 0, 1), (1, blocks + 2, 2, 3)):
                tiles = []
                for k in range(SENT):
                    v = recv_x[side, way, k]
                    v = jnp.where((rows == 0) & has_low, recv_c[side, low_c, k : k + 1], v)
                    v = jnp.where((rows == 7) & has_high, recv_c[side, high_c, k : k + 1], v)
                    tiles.append(v)
                x_index = jnp.minimum(at + a + shift[1, 0], blocks + 2)
                slots[base + 0, at] = jnp.where(zmask, tiles[0], field(0, 0, 0, at - 1))
                slots[base + 1, at] = jnp.where(zmask, tiles[1], field(1, 0, 0, at - 1))
                slots[base + 2, at] = tiles[2]
                slots[base + 3, at] = tiles[3]
                slots[base + 4, at] = jnp.where(
                    zmask, roll_lanes(tiles[1], -1), field(1, 0, 1, at - 1)
                )
                slots[base + 5, at] = jnp.where(
                    zmask, roll_lanes(tiles[0], -1), slots[rel[0, 1, 0], x_index]
                )

            pl.when(has_low)(lambda: margin_rows(side, 0, 0, 0))
            pl.when(has_high)(lambda: margin_rows(side, 0, 1, 7))

            new = list(table)
            for xp in (0, 1):
                for yp in (0, 1):
                    at = xp * 2 + yp
                    same = (a == xp) & (b == yp)
                    x_next = (a != xp) & (b == yp)
                    y_next = (a == xp) & (b != yp)
                    new[at] = jnp.where(same, base, jnp.where(x_next, base + 5, table[at]))
                    new[16 + at] = jnp.where(same, 0, jnp.where(x_next, -a, table[16 + at]))
                    new[4 + at] = jnp.where(same, base + 1, jnp.where(y_next, base + 4, table[4 + at]))
                    new[8 + at] = jnp.where(same, base + 2, table[8 + at])
                    new[12 + at] = jnp.where(same, base + 3, table[12 + at])
            return tuple(new)

        return edge, inner, receive

    table = tuple(jnp.int32(n) for n in range(16)) + tuple(jnp.int32(0) for _ in range(4))
    prepare(0, table)[0]()

    def sweep(s, table):
        _, inner, receive = prepare(s, table)
        inner()
        table = receive()
        prepare(s + 1, table)[0]()
        finish_mid(s)
        return table

    table = lax.fori_loop(0, STEPS - 1, sweep, table)
    _, inner, receive = prepare(STEPS - 1, table)
    inner()
    table = receive()
    finish_mid(STEPS - 1)

    def final(f, xp, yp, block):
        index = block + 1
        if f == 0:
            index = index + table[16 + xp * 2 + yp]
        return slots[table[f * 4 + xp * 2 + yp], index]

    def residual_sums(block, sums):
        sums = list(sums)
        for xp in (0, 1):
            for yp in (0, 1):
                x = 2 * block + xp

                def getter(f, xp=xp, yp=yp):
                    def get(dx, near):
                        at = block + (xp + dx) // 2
                        return final(f, (xp + dx) % 2, yp if near else 1 - yp, at)

                    return get

                ks = coupled(x, yp, [getter(0), getter(1), getter(2)])
                p0 = final(3, xp, yp, block)
                p_x = final(3, 1 - xp, yp, block - 1 + xp)
                p_y = final(3, xp, 1 - yp, block)
                if yp == 0:
                    p_y = roll_rows(p_y, 1)
                before = (p_x, p_y, below_z(p0))
                for d in range(3):
                    u = final(d, xp, yp, block)
                    mom = force[d, x, yp] - (diag[x, yp] * u - ks[d]) - (before[d] - p0)
                    sums[d] = sums[d] + mom
                sums[3] = sums[3] + vis[x, yp]
        return tuple(sums)

    odd_row = (rows & 1) == 1
    packed = []
    for half_no in range(2):
        zero = jnp.zeros(tile, jnp.float32)
        sums = lax.fori_loop(
            half_no * 4 + 1, half_no * 4 + 5, residual_sums, (zero, zero, zero, zero)
        )

        def collect(v):
            v = v + roll_rows(v, -1)
            v = v + roll_lanes(v, -1)
            return v + roll_lanes(v, -2)

        valid = odd_row & (rows < 7) & ((lanes & 3) == 0)
        below = jnp.where(valid, collect(sums[3]), 1.0)
        both = zero
        for d in range(3):
            value = jnp.where(valid, collect(sums[d]) / below, 0.0)
            both = both + (roll_lanes(value, d) if d else value)
        packed.append(both)
    own_part = packed[0] + roll_rows(packed[1], 1)
    shared[...] = own_part
    gathered[0] = own_part

    def spread_copy(hop):
        return pltpu.make_async_remote_copy(
            src_ref=shared,
            dst_ref=gathered.at[hop],
            send_sem=gsend_sem.at[hop],
            recv_sem=grecv_sem.at[hop],
            device_id=(lax.rem(lon + hop, lon_n), lat),
            device_id_type=MESH,
        )

    for hop in range(1, lon_n):
        spread_copy(hop).start()
    for hop in range(1, lon_n):
        spread_copy(hop).wait()

    for part_no in (0, 1):
        for n in range(8):
            guarded(present(n), lambda p=part_no, n=n: first_copy(p, n).wait_send())

    def drain(s, carry):
        for n in range(10):
            guarded(present(n), lambda n=n: copy(n, s).wait_send())
        return carry

    lax.fori_loop(0, STEPS, drain, 0)

    cells = 2 * lon_n
    table_k = cycle_kernel(cells)
    smooth = []
    for half_no in range(2):
        total = jnp.zeros(tile, jnp.float32)
        for hop in range(lon_n):
            odd_k = table_k[(2 * hop + half_no) % cells]
            even_k = table_k[(2 * hop + half_no - 1) % cells]
            total = total + jnp.where(odd_row, odd_k, even_k) * gathered[hop]
        total = GAIN * (total + roll_rows(total, -1))
        per = []
        for d in range(3):
            v = jnp.where(odd_row & ((lanes & 3) == d), total, 0.0)
            if d:
                v = roll_lanes(v, -d)
            v = v + roll_lanes(v, 1)
            v = v + roll_lanes(v, 2)
            per.append(v + roll_rows(v, 1))
        smooth.append(per)

    for half_no in range(2):

        def finish(block, carry, half_no=half_no):
            for xp in (0, 1):
                for yp in (0, 1):
                    x = 2 * block + xp - 2
                    for d in range(3):
                        v = final(d, xp, yp, block) + smooth[half_no][d]
                        for row in range(6):
                            y = 2 * row + yp
                            vel_out[d, x, y : y + 1] = v[row + 1 : row + 2]
                    own = vis[x + 2, yp]
                    v = final(3, xp, yp, block) / jnp.where(own > 0, own, 1.0)
                    for row in range(6):
                        y = 2 * row + yp
                        p_out[x, y : y + 1] = v[row + 1 : row + 2]
            return carry

        lax.fori_loop(half_no * 4 + 1, half_no * 4 + 5, finish, 0)


def body(lon_n, lat_n, velocity, pressure_in, viscosity, body_force, colour_order):
    nx, ny, nz = viscosity.shape
    blocks = nx // 2
    f32 = jnp.float32
    whole = pl.BlockSpec(memory_space=pltpu.VMEM)
    n_slots = FIRST + NEW * STEPS
    return pl.pallas_call(
        functools.partial(kernel, lon_n, lat_n),
        out_shape=(
            jax.ShapeDtypeStruct((3, nx, ny, nz), f32),
            jax.ShapeDtypeStruct((nx, ny, nz), f32),
        ),
        in_specs=[pl.BlockSpec(memory_space=pltpu.SMEM)]
        + [pl.BlockSpec(memory_space=pl.ANY)] * 4,
        out_specs=(whole, whole),
        scratch_shapes=[
            pltpu.VMEM((3, nx, ny, nz), f32),
            pltpu.VMEM((nx, ny, nz), f32),
            pltpu.VMEM((nx, ny, nz), f32),
            pltpu.VMEM((3, nx, ny, nz), f32),
            pltpu.VMEM((nx + 4, 2, 8, nz), f32),
            pltpu.VMEM((3, nx + 4, 2, 8, nz), f32),
            pltpu.VMEM((n_slots, blocks + 3, 8, nz), f32),
            pltpu.VMEM((27, nx + 4, 2, 8, nz), f32),
            pltpu.VMEM((nx + 4, 2, 8, nz), f32),
            pltpu.VMEM((nx + 4, 2, 8, nz), f32),
            pltpu.VMEM((nx + 4, 2, 8, nz), f32),
            pltpu.VMEM((STEPS, 2, SENT, 8, nz), f32),
            pltpu.VMEM((STEPS, 2, NEAR_ROWS, nz), f32),
            pltpu.VMEM((STEPS, 4, 8, nz), f32),
            pltpu.VMEM((STEPS, 2, SENT, 8, nz), f32),
            pltpu.VMEM((STEPS, 2, NEAR_ROWS, nz), f32),
            pltpu.VMEM((STEPS, 4, 8, nz), f32),
            pltpu.VMEM((lon_n, 8, nz), f32),
            pltpu.VMEM((8, nz), f32),
            pltpu.VMEM((2, 2, 12, 8, nz), f32),
            pltpu.VMEM((2, 2, 11, nx, nz), f32),
            pltpu.VMEM((2, 4, 16, nz), f32),
            pltpu.VMEM((2, 2, 12, 8, nz), f32),
            pltpu.VMEM((2, 2, 11, nx, nz), f32),
            pltpu.VMEM((2, 4, 16, nz), f32),
            pltpu.SemaphoreType.DMA((2, 8)),
            pltpu.SemaphoreType.DMA((2, 8)),
            pltpu.VMEM((STEPS, 2, MID_ROWS, nz), f32),
            pltpu.VMEM((STEPS, 2, MID_ROWS, nz), f32),
            pltpu.VMEM((2, blocks + 1, 8, nz), f32),
            pltpu.SemaphoreType.DMA((4,)),
            pltpu.SemaphoreType.DMA((STEPS, 10)),
            pltpu.SemaphoreType.DMA((STEPS, 10)),
            pltpu.SemaphoreType.DMA((lon_n,)),
            pltpu.SemaphoreType.DMA((lon_n,)),
        ],
        compiler_params=pltpu.CompilerParams(
            collective_id=0, has_side_effects=True, vmem_limit_bytes=60 * 1024 * 1024
        ),
        name="vanka",
    )(colour_order, velocity, pressure_in, viscosity, body_force)


def solution(mesh):
    placed = (
        P(None, "lon", "lat", None),
        P("lon", "lat", None),
        P("lon", "lat", None),
        P(None, "lon", "lat", None),
        P(),
    )
    return jax.shard_map(
        functools.partial(body, mesh.shape["lon"], mesh.shape["lat"]),
        mesh=mesh,
        in_specs=placed,
        out_specs=(P(None, "lon", "lat", None), P("lon", "lat", None)),
        check_vma=False,
    )
```

```python
import functools
import math

import jax
import jax.numpy as jnp
from jax import lax
from jax.experimental import pallas as pl
from jax.experimental.pallas import tpu as pltpu
from jax.sharding import PartitionSpec as P

SWEEPS = 2
COLOURS = 8
STEPS = SWEEPS * COLOURS
DAMP = 0.6
GAIN = 0.25
NEAR_ROWS, MID_ROWS = 24, 16
SENT = 4
NEW = 6
FIRST = 16
MESH = pl.DeviceIdType.MESH
DIRECTIONS = ((1, 0), (-1, 0), (0, 1), (0, -1), (1, 1), (1, -1), (-1, 1), (-1, -1), (0, 1), (0, -1))


def opposite(n):
    return DIRECTIONS.index((-DIRECTIONS[n][0], -DIRECTIONS[n][1]))


def kslot(dx, dy, dz):
    return ((dx + 1) * 3 + (dy + 1)) * 3 + (dz + 1)


def cycle_kernel(cells):
    rate = 4.0 / cells
    screening = 2.0 * math.cosh(rate) - 2.0
    factor = screening / (2.0 * math.sinh(rate) * math.sinh(rate * cells / 2.0))
    return [factor * math.cosh(rate * (cells / 2.0 - d)) for d in range(cells)]


def kernel(
    lon_n,
    lat_n,
    order_ref,
    vel_hbm,
    p_hbm,
    vis_hbm,
    force_hbm,
    vel_out,
    p_out,
    vel_in,
    p_in,
    vis_in,
    force_in,
    vis,
    force,
    slots,
    coup,
    diag,
    inv,
    winv,
    send_x,
    send_y,
    send_c,
    recv_x,
    recv_y,
    recv_c,
    gathered,
    shared,
    first_send_x,
    first_send_y,
    first_send_c,
    first_recv_x,
    first_recv_y,
    first_recv_c,
    first_send_sem,
    first_recv_sem,
    send_mid,
    recv_mid,
    pack,
    load_sem,
    send_sem,
    recv_sem,
    gsend_sem,
    grecv_sem,
):
    lon = lax.axis_index("lon")
    lat = lax.axis_index("lat")
    planes = vis.shape[0]
    depth = vis.shape[-1]
    blocks = planes // 2 - 2
    tile = (8, depth)
    rows = lax.broadcasted_iota(jnp.int32, tile, 0)
    lanes = lax.broadcasted_iota(jnp.int32, tile, 1)

    def roll_rows(v, up):
        return pltpu.roll(v, up % 8, 0)

    def roll_lanes(v, up):
        return pltpu.roll(v, up % depth, 1)

    def above_z(v):
        return jnp.where(lanes == depth - 1, 0.0, roll_lanes(v, -1))

    def below_z(v):
        return jnp.where(lanes == 0, 0.0, roll_lanes(v, 1))

    def partner(n):
        dx, dy = DIRECTIONS[n]
        return (lax.rem(lon + dx + lon_n, lon_n), lat + dy)

    def present(n):
        dy = DIRECTIONS[n][1]
        if dy > 0:
            return lat < lat_n - 1
        if dy < 0:
            return lat > 0
        return None

    def guarded(cond, fn):
        if cond is None:
            fn()
        else:
            pl.when(cond)(fn)

    pairs = ((vis_hbm, vis_in), (p_hbm, p_in), (vel_hbm, vel_in), (force_hbm, force_in))
    loads = [pltpu.make_async_copy(src, dst, load_sem.at[n]) for n, (src, dst) in enumerate(pairs)]
    for copy_in in loads:
        copy_in.start()

    barrier = pltpu.get_barrier_semaphore()
    for n in range(8):

        def greet(n=n):
            pl.semaphore_signal(barrier, inc=1, device_id=partner(n), device_id_type=MESH)

        guarded(present(n), greet)
    for hop in range(2, lon_n - 1):
        pl.semaphore_signal(
            barrier, inc=1, device_id=(lax.rem(lon + hop, lon_n), lat), device_id_type=MESH
        )

    blank = jnp.zeros(tile, jnp.float32)

    def clear(x, carry):
        for yp in (0, 1):
            vis[x, yp] = blank
            for d in range(3):
                force[d, x, yp] = blank
        return carry

    lax.fori_loop(0, planes, clear, 0)

    def clear_slots(at, carry):
        for n in range(FIRST):
            slots[n, at] = blank
        return carry

    lax.fori_loop(0, blocks + 3, clear_slots, 0)

    def split(block, carry):
        for xp in (0, 1):
            x = 2 * block + xp - 2
            seen = vis_in[x]
            scaled = p_in[x] * seen
            for y in range(12):
                yp, row = y % 2, y // 2 + 1
                vis[x + 2, yp, row : row + 1] = seen[y : y + 1]
                slots[12 + xp * 2 + yp, block + 1, row : row + 1] = scaled[y : y + 1]
                for d in range(3):
                    slots[d * 4 + xp * 2 + yp, block + 1, row : row + 1] = vel_in[d, x, y : y + 1]
                    force[d, x + 2, yp, row : row + 1] = force_in[d, x, y : y + 1]
        return carry

    for copy_in in loads:
        copy_in.wait()
    lax.fori_loop(1, blocks + 1, split, 0)

    def part(f, x, yp):
        if f == 7:
            return vis.at[x, yp]
        if f >= 4:
            return force.at[f - 4, x, yp]
        return slots.at[f * 4 + (x % 2) * 2 + yp, x // 2 + 1]

    first_x = (
        (
            [(7, 1, yp) for yp in (0, 1)],
            [(7, x, yp) for x in (planes - 2, planes - 1) for yp in (0, 1)],
        ),
        (
            [(f, 1, yp) for f in (0, 1, 2, 3) for yp in (0, 1)],
            [(f, planes - 2, yp) for f in (4, 0, 1, 2, 3) for yp in (0, 1)]
            + [(0, planes - 1, yp) for yp in (0, 1)],
        ),
    )
    first_y = (
        ([(7, 0), (7, 1)], [(7, 0), (7, 1)]),
        (
            [(f, 0) for f in (0, 1, 2, 3)] + [(f, 1) for f in (0, 1, 2, 3, 4, 5, 6)],
            [(f, 0) for f in (0, 1, 2, 3, 5)] + [(1, 1)],
        ),
    )
    own_planes = planes - 4

    def first_copy(part_no, n):
        if n < 2:
            at = (part_no, n, pl.ds(0, len(first_x[part_no][n])))
            src, dst = first_send_x.at[at], first_recv_x.at[at]
        elif n < 4:
            at = (part_no, n - 2, pl.ds(0, len(first_y[part_no][n - 2])))
            src, dst = first_send_y.at[at], first_recv_y.at[at]
        else:
            src, dst = first_send_c.at[part_no, n - 4], first_recv_c.at[part_no, n - 4]
        return pltpu.make_async_remote_copy(
            src_ref=src,
            dst_ref=dst,
            send_sem=first_send_sem.at[part_no, n],
            recv_sem=first_recv_sem.at[part_no, n],
            device_id=partner(n),
            device_id_type=MESH,
        )

    def first_stage(part_no):
        for way in (0, 1):
            for k, (f, x, yp) in enumerate(first_x[part_no][way]):
                source = part(f, x + own_planes if way == 0 else x - own_planes, yp)
                first_send_x[part_no, way, k] = source[...]
                for n in range(4):
                    dx, dy = DIRECTIONS[4 + n]
                    if (dx > 0) == (way == 0):
                        row = 6 if dy > 0 else 1
                        first_send_c[part_no, n, k : k + 1] = source[row : row + 1]
            row = 6 if way == 0 else 1
            for k, (f, yp) in enumerate(first_y[part_no][way]):
                for x in range(own_planes):
                    first_send_y[part_no, way, k, x : x + 1] = part(f, x + 2, yp)[
                        row : row + 1
                    ]

    def first_start(part_no):
        for n in (4, 5, 6, 7, 2, 3, 0, 1):
            guarded(present(n), lambda n=n: first_copy(part_no, n).start())

    has_low = lat > 0
    has_high = lat < lat_n - 1

    def first_finish(part_no):
        for n in range(8):
            guarded(present(opposite(n)), lambda n=n: first_copy(part_no, n).wait_recv())
        for way in (0, 1):
            low_c, high_c = (0, 1) if way == 0 else (2, 3)
            for k, (f, x, yp) in enumerate(first_x[part_no][way]):
                v = first_recv_x[part_no, way, k]
                v = jnp.where((rows == 0) & has_low, first_recv_c[part_no, low_c, k : k + 1], v)
                v = jnp.where((rows == 7) & has_high, first_recv_c[part_no, high_c, k : k + 1], v)
                part(f, x, yp)[...] = v

        def first_rows(way, row):
            for k, (f, yp) in enumerate(first_y[part_no][way]):
                for x in range(own_planes):
                    part(f, x + 2, yp)[row : row + 1] = first_recv_y[
                        part_no, way, k, x : x + 1
                    ]

        pl.when(has_low)(lambda: first_rows(0, 0))
        pl.when(has_high)(lambda: first_rows(1, 7))

    first_stage(0)
    ends = (lat == 0).astype(jnp.int32) + (lat == lat_n - 1).astype(jnp.int32)
    pl.semaphore_wait(barrier, lon_n + 5 - 3 * ends)
    first_start(0)
    first_stage(1)
    first_start(1)
    first_finish(0)

    def inside(yp):
        y = lat * 12 + 2 * (rows - 1) + yp
        return (y >= 0) & (y < 12 * lat_n)

    half = [(1, dy, dz) for dy in (-1, 0, 1) for dz in (-1, 0, 1)]
    half += [(0, 1, dz) for dz in (-1, 0, 1)] + [(0, 0, 1)]

    def couple(x, carry):
        for yp in (0, 1):
            own = vis[x, yp]
            for dx in (0, 1):
                for dy in (-1, 0, 1):
                    offsets = [o for o in half if o[0] == dx and o[1] == dy]
                    if not offsets:
                        continue
                    other_yp = yp if dy == 0 else 1 - yp
                    shift = 0
                    if dy == 1 and yp == 1:
                        shift = -1
                    if dy == -1 and yp == 0:
                        shift = 1
                    other = vis[x + dx, other_yp]
                    if shift:
                        other = roll_rows(other, shift)
                    for o in offsets:
                        dz = o[2]
                        beside = other
                        if dz == 1:
                            beside = above_z(other)
                        elif dz == -1:
                            beside = below_z(other)
                        reach = abs(dx) + abs(dy) + abs(dz)
                        scale = 2.0 * 0.5 ** (reach - 1)
                        value = (scale * own) * beside / jnp.maximum(own + beside, 1.0)
                        coup[kslot(*o), x, yp] = value
                        back = value
                        if dz:
                            back = roll_lanes(back, dz)
                        if shift:
                            back = roll_rows(back, -shift)
                        coup[kslot(-dx, -dy, -dz), x + dx, other_yp] = back
        return carry

    lax.fori_loop(1, planes - 1, couple, 0)

    def diagonal(x, carry):
        for yp in (0, 1):
            total = jnp.zeros(tile, jnp.float32)
            for n in range(27):
                if n != 13:
                    total = total + coup[n, x, yp]
            diag[x, yp] = total
            ok = inside(yp) & (total > 0)
            inv[x, yp] = jnp.where(ok, 1.0 / jnp.where(ok, total, 1.0), 0.0)
        return carry

    lax.fori_loop(2, planes - 1, diagonal, 0)

    def weights(x, carry):
        for yp in (0, 1):
            own = inv[x, yp]
            up = inv[x, 1 - yp]
            if yp == 1:
                up = roll_rows(up, -1)
            total = 3.0 * own + inv[x + 1, yp] + up + above_z(own)
            ok = inside(yp) & (total > 0)
            winv[x, yp] = jnp.where(ok, 1.0 / jnp.where(ok, total, 1.0), 0.0)
        return carry

    lax.fori_loop(2, planes - 2, weights, 0)
    first_finish(1)

    def coupled(x, t, fields):
        at_low = t == 0

        def turn(v):
            return jnp.where(at_low, roll_rows(v, 1), roll_rows(v, -1))

        sums = [[None] * 3 for _ in fields]

        def gather(dy, yp, near):
            for dx in (-1, 0, 1):
                tiles = [f(dx, near) for f in fields]
                for dz in (-1, 0, 1):
                    if near and dx == 0 and dz == 0:
                        continue
                    k = coup[((1 - dx) * 3 + (1 - dy)) * 3 + (1 - dz), x + dx, yp]
                    for n, v in enumerate(tiles):
                        term = k * v
                        old = sums[n][dz + 1]
                        sums[n][dz + 1] = term if old is None else old + term

        gather(jnp.where(at_low, -1, 1), 1 - t, 0)
        for n in range(len(fields)):
            sums[n] = [turn(v) for v in sums[n]]
        gather(jnp.where(at_low, 1, -1), 1 - t, 0)
        gather(0, t, 1)
        return [s[1] + roll_lanes(s[2], -1) + roll_lanes(s[0], 1) for s in sums]

    def pick(table, xp, yp):
        low = jnp.where(yp == 0, table[0], table[1])
        high = jnp.where(yp == 0, table[2], table[3])
        return jnp.where(xp == 0, low, high)

    def copy(n, side):
        if n < 2:
            src, dst = send_x.at[side, n], recv_x.at[side, n]
        elif n < 4:
            src, dst = send_y.at[side, n - 2], recv_y.at[side, n - 2]
        elif n >= 8:
            src, dst = send_mid.at[side, n - 8], recv_mid.at[side, n - 8]
        else:
            src, dst = send_c.at[side, n - 4], recv_c.at[side, n - 4]
        return pltpu.make_async_remote_copy(
            src_ref=src,
            dst_ref=dst,
            send_sem=send_sem.at[side, n],
            recv_sem=recv_sem.at[side, n],
            device_id=partner(n),
            device_id_type=MESH,
        )

    near = (1, 2, blocks - 2, blocks - 1, blocks)
    mid = tuple(range(3, blocks - 2))

    def margin_rows(side, which, way, row):
        base = FIRST + NEW * side
        z_parity = (order_ref[lax.rem(side, COLOURS)] >> 2) & 1
        zrow = (lanes[0:1] & 1) == z_parity
        buffer, group = (recv_y, near) if which == 0 else (recv_mid, mid)
        per = len(group)
        got = buffer[side, way]
        turned = roll_lanes(got[0:16], -1)
        for k, v, at, mixed in (
            (0, got, 0, True),
            (1, got, per, True),
            (2, got, 2 * per, False),
            (3, got, 3 * per, False),
            (4, turned, per, True),
            (5, turned, 0, True),
        ):
            for n, block in enumerate(group):
                new_row = v[at + n : at + n + 1]
                if mixed:
                    new_row = jnp.where(zrow, new_row, slots[base + k, block + 1, row : row + 1])
                slots[base + k, block + 1, row : row + 1] = new_row

    def finish_mid(side):
        for n in (8, 9):
            guarded(present(opposite(n)), lambda n=n: copy(n, side).wait_recv())
        pl.when(has_low)(lambda: margin_rows(side, 1, 0, 0))
        pl.when(has_high)(lambda: margin_rows(side, 1, 1, 7))

    def prepare(s, table):
        colour = order_ref[lax.rem(s, COLOURS)]
        a = colour & 1
        b = (colour >> 1) & 1
        c = (colour >> 2) & 1
        base = FIRST + NEW * s
        side = s
        rel = {}
        for f in range(4):
            for xr in (0, 1):
                for yr in (0, 1):
                    rel[f, xr, yr] = pick(table[f * 4 : f * 4 + 4], a ^ xr, b ^ yr)
        shift = {
            (xr, yr): pick(table[16:20], a ^ xr, b ^ yr) for xr in (0, 1) for yr in (0, 1)
        }

        def field(f, xr, yr, block):
            index = block + 1
            if f == 0:
                index = index + shift[xr, yr]
            return slots[rel[f, xr, yr], index]

        zmask = (lanes & 1) == c
        z3 = (lanes > 0) | (c == 0)
        ymask = lat * 12 + 2 * (rows - 1) + (1 - b) >= 1
        low = b == 0

        def block_step(block, carry):
            x = 2 * block + a

            def main(f):
                def get(dx, near):
                    at = block if dx == 0 else (block - 1 + a if dx < 0 else block + a)
                    return field(f, abs(dx), 0 if near else 1, at)

                return get

            def xprime(dx, near):
                at = block + a if dx == 0 else (block if dx < 0 else block + 1)
                return field(0, 1 - abs(dx), 0 if near else 1, at)

            def yprime(dx, near):
                at = block if dx == 0 else (block - 1 + a if dx < 0 else block + a)
                return field(1, abs(dx), 1 if near else 0, at)

            p0 = field(3, 0, 0, block)
            p_x = field(3, 1, 0, block - 1 + a)
            p_x1 = field(3, 1, 0, block + a)
            p_y1 = field(3, 0, 1, block)
            k1, k2, k3 = coupled(x, b, [main(0), main(1), main(2)])
            own_inv = inv[x, b]
            p_y = jnp.where(low, roll_rows(p_y1, 1), p_y1)
            g1 = own_inv * (force[0, x, b] + k1 + (p0 - p_x))
            g2 = own_inv * (force[1, x, b] + k2 + (p0 - p_y))
            g3 = own_inv * (force[2, x, b] + k3 + (p0 - below_z(p0)))
            (kx,) = coupled(x + 1, b, [xprime])
            inv_x = inv[x + 1, b]
            gx = inv_x * (force[0, x + 1, b] + kx + (p_x1 - p0))
            (ky,) = coupled(x, 1 - b, [yprime])
            inv_y = inv[x, 1 - b]
            gy = inv_y * (force[1, x, 1 - b] + ky + (p_y1 - jnp.where(low, p0, roll_rows(p0, 1))))
            spread = (gx - g1) + (jnp.where(low, gy, roll_rows(gy, -1)) - g2) + (above_z(g3) - g3)
            dp = jnp.where(zmask, spread * winv[x, b], 0.0)
            dp_y = jnp.where(low, dp, roll_rows(dp, 1))
            keep = 1.0 - DAMP
            u1 = field(0, 0, 0, block)
            u2 = field(1, 0, 0, block)
            u3 = field(2, 0, 0, block)
            ux = field(0, 1, 0, block + a)
            uy = field(1, 0, 1, block)
            push = own_inv * dp
            new_1 = jnp.where(zmask, keep * u1 + DAMP * (g1 + push), u1)
            new_2 = jnp.where(zmask, keep * u2 + DAMP * (g2 + push), u2)
            new_y = jnp.where(zmask & ymask, keep * uy + DAMP * (gy - inv_y * dp_y), uy)
            new_x = jnp.where(zmask, keep * ux + DAMP * (gx - inv_x * dp), ux)
            slots[base + 0, block + 1] = new_1
            slots[base + 1, block + 1] = new_2
            pack[0, block] = jnp.where(zmask, new_1, roll_lanes(new_x, 1))
            pack[1, block] = jnp.where(zmask, new_2, roll_lanes(new_y, 1))
            slots[base + 2, block + 1] = jnp.where(
                z3, keep * u3 + DAMP * (g3 + own_inv * (dp - below_z(dp))), u3
            )
            slots[base + 3, block + 1] = p0 + DAMP * dp
            slots[base + 4, block + 1] = new_y
            slots[base + 5, block + 1] = new_x
            return carry

        def packed_tile(k, block):
            return pack.at[k, block] if k < 2 else slots.at[base + k, block + 1]

        def edge():
            block_step(1, 0)
            block_step(blocks, 0)

            for k in range(SENT):
                send_x[side, 0, k] = packed_tile(k, blocks)[...]
                send_x[side, 1, k] = packed_tile(k, 1)[...]
                for n in range(4):
                    dx, dy = DIRECTIONS[4 + n]
                    row = 6 if dy > 0 else 1
                    source = packed_tile(k, blocks if dx > 0 else 1)
                    send_c[side, n, k : k + 1] = source[row : row + 1]
            for n in (4, 5, 6, 7, 0, 1):
                guarded(present(n), lambda n=n: copy(n, side).start())

        def inner():
            for block in (2, blocks - 2, blocks - 1):
                block_step(block, 0)

            def stage_rows(buffer, group):
                for k in range(SENT):
                    for n, block in enumerate(group):
                        at = k * len(group) + n
                        source = packed_tile(k, block)
                        buffer[side, 0, at : at + 1] = source[6:7]
                        buffer[side, 1, at : at + 1] = source[1:2]

            stage_rows(send_y, near)
            for n in (2, 3):
                guarded(present(n), lambda n=n: copy(n, side).start())
            for block in mid:
                block_step(block, 0)
            stage_rows(send_mid, mid)
            for n in (8, 9):
                guarded(present(n), lambda n=n: copy(n, side).start())

        def receive():
            for n in range(8):
                guarded(present(opposite(n)), lambda n=n: copy(n, side).wait_recv())

            for way, at, low_c, high_c in ((0, 1, 0, 1), (1, blocks + 2, 2, 3)):
                tiles = []
                for k in range(SENT):
                    v = recv_x[side, way, k]
                    v = jnp.where((rows == 0) & has_low, recv_c[side, low_c, k : k + 1], v)
                    v = jnp.where((rows == 7) & has_high, recv_c[side, high_c, k : k + 1], v)
                    tiles.append(v)
                x_index = jnp.minimum(at + a + shift[1, 0], blocks + 2)
                slots[base + 0, at] = jnp.where(zmask, tiles[0], field(0, 0, 0, at - 1))
                slots[base + 1, at] = jnp.where(zmask, tiles[1], field(1, 0, 0, at - 1))
                slots[base + 2, at] = tiles[2]
                slots[base + 3, at] = tiles[3]
                slots[base + 4, at] = jnp.where(
                    zmask, roll_lanes(tiles[1], -1), field(1, 0, 1, at - 1)
                )
                slots[base + 5, at] = jnp.where(
                    zmask, roll_lanes(tiles[0], -1), slots[rel[0, 1, 0], x_index]
                )

            pl.when(has_low)(lambda: margin_rows(side, 0, 0, 0))
            pl.when(has_high)(lambda: margin_rows(side, 0, 1, 7))

            new = list(table)
            for xp in (0, 1):
                for yp in (0, 1):
                    at = xp * 2 + yp
                    same = (a == xp) & (b == yp)
                    x_next = (a != xp) & (b == yp)
                    y_next = (a == xp) & (b != yp)
                    new[at] = jnp.where(same, base, jnp.where(x_next, base + 5, table[at]))
                    new[16 + at] = jnp.where(same, 0, jnp.where(x_next, -a, table[16 + at]))
                    new[4 + at] = jnp.where(same, base + 1, jnp.where(y_next, base + 4, table[4 + at]))
                    new[8 + at] = jnp.where(same, base + 2, table[8 + at])
                    new[12 + at] = jnp.where(same, base + 3, table[12 + at])
            return tuple(new)

        return edge, inner, receive

    table = tuple(jnp.int32(n) for n in range(16)) + tuple(jnp.int32(0) for _ in range(4))
    prepare(0, table)[0]()

    def sweep(s, table):
        _, inner, receive = prepare(s, table)
        inner()
        table = receive()
        prepare(s + 1, table)[0]()
        finish_mid(s)
        return table

    table = lax.fori_loop(0, STEPS - 1, sweep, table)
    _, inner, receive = prepare(STEPS - 1, table)
    inner()
    table = receive()
    finish_mid(STEPS - 1)

    def final(f, xp, yp, block):
        index = block + 1
        if f == 0:
            index = index + table[16 + xp * 2 + yp]
        return slots[table[f * 4 + xp * 2 + yp], index]

    def residual_sums(block, sums):
        sums = list(sums)
        for xp in (0, 1):
            for yp in (0, 1):
                x = 2 * block + xp

                def getter(f, xp=xp, yp=yp):
                    def get(dx, near):
                        at = block + (xp + dx) // 2
                        return final(f, (xp + dx) % 2, yp if near else 1 - yp, at)

                    return get

                ks = coupled(x, yp, [getter(0), getter(1), getter(2)])
                p0 = final(3, xp, yp, block)
                p_x = final(3, 1 - xp, yp, block - 1 + xp)
                p_y = final(3, xp, 1 - yp, block)
                if yp == 0:
                    p_y = roll_rows(p_y, 1)
                before = (p_x, p_y, below_z(p0))
                for d in range(3):
                    u = final(d, xp, yp, block)
                    mom = force[d, x, yp] - (diag[x, yp] * u - ks[d]) - (before[d] - p0)
                    sums[d] = sums[d] + mom
                sums[3] = sums[3] + vis[x, yp]
        return tuple(sums)

    odd_row = (rows & 1) == 1
    packed = []
    for half_no in range(2):
        zero = jnp.zeros(tile, jnp.float32)
        sums = lax.fori_loop(
            half_no * 4 + 1, half_no * 4 + 5, residual_sums, (zero, zero, zero, zero)
        )

        def collect(v):
            v = v + roll_rows(v, -1)
            v = v + roll_lanes(v, -1)
            return v + roll_lanes(v, -2)

        valid = odd_row & (rows < 7) & ((lanes & 3) == 0)
        below = jnp.where(valid, collect(sums[3]), 1.0)
        both = zero
        for d in range(3):
            value = jnp.where(valid, collect(sums[d]) / below, 0.0)
            both = both + (roll_lanes(value, d) if d else value)
        packed.append(both)
    own_part = packed[0] + roll_rows(packed[1], 1)
    shared[...] = own_part
    gathered[0] = own_part

    def spread_copy(hop):
        return pltpu.make_async_remote_copy(
            src_ref=shared,
            dst_ref=gathered.at[hop],
            send_sem=gsend_sem.at[hop],
            recv_sem=grecv_sem.at[hop],
            device_id=(lax.rem(lon + hop, lon_n), lat),
            device_id_type=MESH,
        )

    for hop in range(1, lon_n):
        spread_copy(hop).start()
    for hop in range(1, lon_n):
        spread_copy(hop).wait()

    for part_no in (0, 1):
        for n in range(8):
            guarded(present(n), lambda p=part_no, n=n: first_copy(p, n).wait_send())

    def drain(s, carry):
        for n in range(10):
            guarded(present(n), lambda n=n: copy(n, s).wait_send())
        return carry

    lax.fori_loop(0, STEPS, drain, 0)

    cells = 2 * lon_n
    table_k = cycle_kernel(cells)
    smooth = []
    for half_no in range(2):
        total = jnp.zeros(tile, jnp.float32)
        for hop in range(lon_n):
            odd_k = table_k[(2 * hop + half_no) % cells]
            even_k = table_k[(2 * hop + half_no - 1) % cells]
            total = total + jnp.where(odd_row, odd_k, even_k) * gathered[hop]
        total = GAIN * (total + roll_rows(total, -1))
        per = []
        for d in range(3):
            v = jnp.where(odd_row & ((lanes & 3) == d), total, 0.0)
            if d:
                v = roll_lanes(v, -d)
            v = v + roll_lanes(v, 1)
            v = v + roll_lanes(v, 2)
            per.append(v + roll_rows(v, 1))
        smooth.append(per)

    for half_no in range(2):

        def finish(block, carry, half_no=half_no):
            for xp in (0, 1):
                for yp in (0, 1):
                    x = 2 * block + xp - 2
                    for d in range(3):
                        v = final(d, xp, yp, block) + smooth[half_no][d]
                        for row in range(6):
                            y = 2 * row + yp
                            vel_out[d, x, y : y + 1] = v[row + 1 : row + 2]
                    own = vis[x + 2, yp]
                    v = final(3, xp, yp, block) / jnp.where(own > 0, own, 1.0)
                    for row in range(6):
                        y = 2 * row + yp
                        p_out[x, y : y + 1] = v[row + 1 : row + 2]
            return carry

        lax.fori_loop(half_no * 4 + 1, half_no * 4 + 5, finish, 0)


def body(lon_n, lat_n, velocity, pressure_in, viscosity, body_force, colour_order):
    nx, ny, nz = viscosity.shape
    blocks = nx // 2
    f32 = jnp.float32
    whole = pl.BlockSpec(memory_space=pltpu.VMEM)
    n_slots = FIRST + NEW * STEPS
    return pl.pallas_call(
        functools.partial(kernel, lon_n, lat_n),
        out_shape=(
            jax.ShapeDtypeStruct((3, nx, ny, nz), f32),
            jax.ShapeDtypeStruct((nx, ny, nz), f32),
        ),
        in_specs=[pl.BlockSpec(memory_space=pltpu.SMEM)]
        + [pl.BlockSpec(memory_space=pl.ANY)] * 4,
        out_specs=(whole, whole),
        scratch_shapes=[
            pltpu.VMEM((3, nx, ny, nz), f32),
            pltpu.VMEM((nx, ny, nz), f32),
            pltpu.VMEM((nx, ny, nz), f32),
            pltpu.VMEM((3, nx, ny, nz), f32),
            pltpu.VMEM((nx + 4, 2, 8, nz), f32),
            pltpu.VMEM((3, nx + 4, 2, 8, nz), f32),
            pltpu.VMEM((n_slots, blocks + 3, 8, nz), f32),
            pltpu.VMEM((27, nx + 4, 2, 8, nz), f32),
            pltpu.VMEM((nx + 4, 2, 8, nz), f32),
            pltpu.VMEM((nx + 4, 2, 8, nz), f32),
            pltpu.VMEM((nx + 4, 2, 8, nz), f32),
            pltpu.VMEM((STEPS, 2, SENT, 8, nz), f32),
            pltpu.VMEM((STEPS, 2, NEAR_ROWS, nz), f32),
            pltpu.VMEM((STEPS, 4, 8, nz), f32),
            pltpu.VMEM((STEPS, 2, SENT, 8, nz), f32),
            pltpu.VMEM((STEPS, 2, NEAR_ROWS, nz), f32),
            pltpu.VMEM((STEPS, 4, 8, nz), f32),
            pltpu.VMEM((lon_n, 8, nz), f32),
            pltpu.VMEM((8, nz), f32),
            pltpu.VMEM((2, 2, 12, 8, nz), f32),
            pltpu.VMEM((2, 2, 11, nx, nz), f32),
            pltpu.VMEM((2, 4, 16, nz), f32),
            pltpu.VMEM((2, 2, 12, 8, nz), f32),
            pltpu.VMEM((2, 2, 11, nx, nz), f32),
            pltpu.VMEM((2, 4, 16, nz), f32),
            pltpu.SemaphoreType.DMA((2, 8)),
            pltpu.SemaphoreType.DMA((2, 8)),
            pltpu.VMEM((STEPS, 2, MID_ROWS, nz), f32),
            pltpu.VMEM((STEPS, 2, MID_ROWS, nz), f32),
            pltpu.VMEM((2, blocks + 1, 8, nz), f32),
            pltpu.SemaphoreType.DMA((4,)),
            pltpu.SemaphoreType.DMA((STEPS, 10)),
            pltpu.SemaphoreType.DMA((STEPS, 10)),
            pltpu.SemaphoreType.DMA((lon_n,)),
            pltpu.SemaphoreType.DMA((lon_n,)),
        ],
        compiler_params=pltpu.CompilerParams(
            collective_id=0, has_side_effects=True, vmem_limit_bytes=60 * 1024 * 1024
        ),
        name="vanka",
    )(colour_order, velocity, pressure_in, viscosity, body_force)


def solution(mesh):
    placed = (
        P(None, "lon", "lat", None),
        P("lon", "lat", None),
        P("lon", "lat", None),
        P(None, "lon", "lat", None),
        P(),
    )
    return jax.shard_map(
        functools.partial(body, mesh.shape["lon"], mesh.shape["lat"]),
        mesh=mesh,
        in_specs=placed,
        out_specs=(P(None, "lon", "lat", None), P("lon", "lat", None)),
        check_vma=False,
    )
```
